32 devices in a mesh: seq: 8 (over y, x, core), wsh: 4 (over z).
Axes of the slice: x: 2, y: 2, z: 4, core: 2. Of those that a mesh axis runs over, the one named last changes fastest.
Arguments:
- x_in: bfloat16 [4, 4096, 1024], P('wsh', 'seq'), may hold values from -6 to 6
- seg_ids: int32 [4, 4096], P('wsh', 'seq'), may hold values from 0 to 7, never falling along the last dimension, each value on 1 to 2048 neighbouring positions
- in_weight: bfloat16 [1024, 4384], P('wsh'), may hold values from -0.1875 to 0.1875
- out_weight: bfloat16 [2048, 1024], P('wsh'), may hold values from -0.125 to 0.125
- conv_weight: bfloat16 [4, 2304], P(None, 'wsh'), may hold values from -3 to 3
- conv_bias: bfloat16 [2304], P('wsh'), may hold values from -0.5 to 0.5
- dt_bias: bfloat16 [32], P('wsh'), may hold values from -6 to -3
- a_log: bfloat16 [32], P('wsh'), may hold values from -4 to 1.5
- skip_gain: bfloat16 [32], P('wsh'), may hold values from 0.5 to 1.5
- norm_gain: bfloat16 [1024], P('wsh'), may hold values from 0.5 to 1.5
- gate_gain: bfloat16 [2048], P('wsh'), may hold values from 0.5 to 1.5
- cotangent: bfloat16 [4, 4096, 1024], P('wsh', 'seq'), may hold values from -6 to 6
Outputs:
- output: bfloat16 [4, 4096, 1024], P('wsh', 'seq')
- grad_input: float32 [4, 4096, 1024], P('wsh', 'seq')
- grad_in_weight: float32 [1024, 4384], P('wsh')
- grad_out_weight: float32 [2048, 1024], P('wsh')
- grad_conv_weight: float32 [4, 2304], P(None, 'wsh')
- grad_conv_bias: float32 [2304], P('wsh')
- grad_dt_bias: float32 [32], P('wsh')
- grad_a_log: float32 [32], P('wsh')
- grad_skip: float32 [32], P('wsh')
- grad_norm_gain: float32 [1024], P('wsh')
- grad_gate_gain: float32 [2048], P('wsh')
The draws below stay inside these ranges and needn't reach their ends.
Inputs may be any that keep to these rules, and one draw needn't show every extreme that they name: `seg_ids`: in each stream, document numbers never fall, each document has 1 to 2048 rows and one has exactly 2048.
All inputs are finite; a program needn't handle non-finite values.
Results may differ from the reference program's by a relative error of at most 0.012.
The reference program's roundings to bfloat16 on the way count: a program that leaves them out, or rounds other values in their place, can miss the bound.
Values may be sent and summed in bfloat16 or wider, within the bound.
No kernel may reach another device: no remote copies, remote signals or barrier semaphores. Data moves between devices by JAX's collectives and lax.ppermute only.
A program may use at most 192 MiB of HBM per device.

```python
import math
import jax
import jax.numpy as jnp
import numpy as np
from jax import lax

D = 1024
H = 32
K = 4
BLOCK = 512
DOC_MOST = 2048
DOC_MEAN = 512
DI = 2048
CH = 2304
E = 4384
LENGTH = 4096
STREAMS = 4


def level_of(rng, dims, cuts, low, high):
    gain, own = 1.0, jax.random.fold_in(rng, 6)
    for dim, parts in cuts:
        steps = jnp.exp(jax.random.uniform(jax.random.fold_in(own, dim), (parts,), jnp.float32, low / len(cuts), high / len(cuts)))
        gain = gain * jnp.repeat(steps, dims[dim] // parts).reshape([-1 if axis == dim else 1 for axis in range(len(dims))])
    return gain


def profile(amount, total, limit, skew):
    loads = [(1 << 20) // math.isqrt(standing ** skew) + 1 for standing in range(2, amount + 1)]
    spare, holding = total - limit - (amount - 1), [1] * (amount - 1)
    while spare > 0:
        movable = [i for i in range(amount - 1) if holding[i] < limit]
        whole, remaining = sum([loads[i] for i in movable]), spare
        for i in movable:
            extra = min(limit - holding[i], max(1, remaining * loads[i] // whole), spare)
            holding[i] = holding[i] + extra
            spare = spare - extra
    return np.array([limit] + holding)


def ragged_sizes(stream_key, number_of, total, reach, slope):
    if number_of == 2:
        one = jax.random.randint(stream_key, (), max(1, total - reach), min(reach, total - 1) + 1)
        return jnp.stack([one, total - one])
    sizes = jnp.asarray(profile(number_of, total, reach, slope), jnp.int32)
    pairs = (number_of - 1) // 2
    source_of, taker = sizes[1:1 + 2 * pairs:2], sizes[2:2 + 2 * pairs:2]
    room = jnp.minimum(source_of - 1, reach - taker)
    passed = jax.random.randint(jax.random.fold_in(stream_key, 1), (pairs,), 0, 1 << 20) % (room + 1)
    sizes = sizes.at[1:1 + 2 * pairs:2].set(source_of - passed).at[2:2 + 2 * pairs:2].set(taker + passed)
    return sizes[jax.random.permutation(jax.random.fold_in(stream_key, 2), number_of)]


def bell_draw(key, extent, deviation, most, shards=(), kind=jnp.bfloat16):
    values = jax.random.normal(key, extent, jnp.float32) * deviation
    if len(shards) > 0:
        values = level_of(key, extent, shards, -0.22, 0.18) * values
    return jnp.clip(values, min=-most, max=most).astype(kind)


def setup_inputs(seed: int = 0) -> dict:
    splits = jax.random.split(jax.random.key(seed), 13)
    return {
        "x_in": bell_draw(splits[0], (STREAMS, LENGTH, D), 1.0, 6.0, ((0, 4), (1, 8))),
        "seg_ids": jax.vmap(lambda own: jnp.searchsorted(jnp.cumsum(ragged_sizes(own, LENGTH // DOC_MEAN, LENGTH, DOC_MOST, 1)), jnp.arange(LENGTH), side="right"))(jax.random.split(splits[1], STREAMS)).reshape((STREAMS, LENGTH)).astype(jnp.int32),
        "in_weight": bell_draw(splits[2], (D, E), D ** -0.5, 0.1875, ((0, 4),)),
        "out_weight": bell_draw(splits[3], (DI, D), DI ** -0.5, 0.125, ((0, 4),)),
        "conv_weight": bell_draw(splits[4], (K, CH), K ** -0.5, 3.0, ((1, 4),)),
        "conv_bias": jnp.clip(jax.random.uniform(splits[5], (CH,), jnp.float32, -0.5, 0.5) * level_of(splits[5], (CH,), ((0, 4),), -0.4, 0.0), -0.5, 0.5).astype(jnp.bfloat16),
        "dt_bias": jnp.clip(-6.0 + 3.0 * jax.random.uniform(splits[6], (H,), jnp.float32) ** level_of(splits[6], (H,), ((0, 4),), -0.2, 0.2), -6.0, -3.0).astype(jnp.bfloat16),
        "a_log": jnp.clip(-4.0 + 5.5 * jax.random.uniform(splits[7], (H,), jnp.float32) ** level_of(splits[7], (H,), ((0, 4),), -0.2, 0.2), -4.0, 1.5).astype(jnp.bfloat16),
        "skip_gain": jnp.clip(0.5 + 1.0 * jax.random.uniform(splits[8], (H,), jnp.float32) ** level_of(splits[8], (H,), ((0, 4),), -0.2, 0.2), 0.5, 1.5).astype(jnp.bfloat16),
        "norm_gain": jnp.clip(1.0 + 0.1 * jax.random.normal(splits[9], (D,), jnp.float32), 0.5, 1.5).astype(jnp.bfloat16),
        "gate_gain": jnp.clip(1.0 + 0.1 * jax.random.normal(splits[10], (DI,), jnp.float32), 0.5, 1.5).astype(jnp.bfloat16),
        "cotangent": bell_draw(splits[11], (STREAMS, LENGTH, D), 1.0, 6.0, ((0, 4), (1, 8))),
    }


@jax.custom_vjp
def low(v):
    return lax.optimization_barrier(v.astype(jnp.bfloat16)).astype(jnp.float32)

@jax.custom_vjp
def low_back(v):
    return v

def low_keep(v):
    return (low(v), None)

def low_pass(kept, grad):
    return (grad,)

def back_keep(v):
    return (v, None)

def back_low(kept, grad):
    return (low(grad),)
low.defvjp(low_keep, low_pass)
low_back.defvjp(back_keep, back_low)
epsilon = 1e-05
highest = lax.Precision.HIGHEST

def rms_scale(values, gain_vec):
    return values * lax.rsqrt(lax.optimization_barrier(jnp.mean(values * values, axis=-1, keepdims=True)) + epsilon) * gain_vec

def gated_norm(scanned, gate_part, gain_vec):
    return rms_scale(scanned * jax.nn.silu(gate_part), gain_vec)

def conv_silu(extended, ext_ids, conv_weight, conv_bias):
    tap_count = conv_weight.shape[0]
    rows_count = extended.shape[0] - tap_count + 1
    current = ext_ids[tap_count - 1:]
    summed = jnp.zeros((rows_count, extended.shape[1]), jnp.float32) + conv_bias[None, :]
    for offset in range(tap_count):
        window = extended[offset:offset + rows_count]
        matching = (ext_ids[offset:offset + rows_count] == current).astype(jnp.float32)
        summed = summed + window * conv_weight[offset][None, :] * matching[:, None]
    return jax.nn.silu(summed)

def scan_heads(head_x, head_dt, b_rows, c_rows, segment_ids, dt_bias, a_log, skip_gain, block_rows):
    length = head_x.shape[0]
    head_count = head_dt.shape[1]
    head_dim = head_x.shape[1] // head_count
    state_dim = b_rows.shape[1]
    blocks = length // block_rows
    step_size = jax.nn.softplus(head_dt + dt_bias[None, :])
    log_decay = -jnp.exp(a_log)[None, :] * step_size
    x_heads = head_x.reshape(length, head_count, head_dim)
    scaled = x_heads * step_size[:, :, None]
    prev_ids = jnp.concatenate([jnp.full((1,), -1, jnp.int32), segment_ids[block_rows - 1::block_rows][:-1].astype(jnp.int32)])
    lower_mask = jnp.tril(jnp.ones((block_rows, block_rows), jnp.bool_))

    def one_block(carry_state, pieces):
        decay_part, scaled_part, b_part, c_part, id_part, prev_id = pieces
        cumulative = jnp.cumsum(decay_part, axis=0)
        linked = (id_part[:, None] == id_part[None, :]) & lower_mask
        differ = cumulative.T[:, :, None] - cumulative.T[:, None, :]
        kernel = jnp.where(linked[None], jnp.exp(jnp.where(linked[None], differ, 0.0)), 0.0)
        scores = jnp.dot(c_part, b_part.T, precision=highest)
        mixed_kernel = kernel * scores[None]
        intra_out = jnp.einsum('hts,shp->thp', mixed_kernel, scaled_part, precision=highest)
        carried = (id_part == prev_id).astype(jnp.float32)
        carry_in = jnp.exp(cumulative) * carried[:, None]
        inter_out = jnp.einsum('tn,hpn->thp', c_part, carry_state, precision=highest) * carry_in[:, :, None]
        end_link = (id_part == id_part[-1]).astype(jnp.float32)
        to_end = jnp.exp(cumulative[-1][None, :] - cumulative) * end_link[:, None]
        fresh = jnp.einsum('shp,sn->hpn', to_end[:, :, None] * scaled_part, b_part, precision=highest)
        block_decay = jnp.exp(cumulative[-1]) * carried[-1]
        new_state = carry_state * block_decay[:, None, None] + fresh
        return (new_state, intra_out + inter_out)
    pieces = (log_decay.reshape(blocks, block_rows, head_count), scaled.reshape(blocks, block_rows, head_count, head_dim), b_rows.reshape(blocks, block_rows, state_dim), c_rows.reshape(blocks, block_rows, state_dim), segment_ids.reshape(blocks, block_rows), prev_ids)
    initial = jnp.zeros((head_count, head_dim, state_dim), jnp.float32)
    ignored, outputs = lax.scan(jax.checkpoint(one_block), initial, pieces)
    result = outputs.reshape(length, head_count, head_dim) + skip_gain[None, :, None] * x_heads
    return result.reshape(length, head_count * head_dim)

def stream_forward(residual_in, doc_ids, weight_set):
    in_weight, out_weight, conv_weight, conv_bias, dt_bias, a_log, skip_gain, norm_gain, gate_gain = weight_set
    inner_width = out_weight.shape[0]
    head_count = dt_bias.shape[0]
    state_dim = (in_weight.shape[1] - 2 * inner_width - head_count) // 2
    channels = inner_width + 2 * state_dim
    tap_count = conv_weight.shape[0]
    normed = low(rms_scale(residual_in, norm_gain))
    projected = low_back(low(jnp.dot(normed, in_weight, precision=highest)))
    gate_part = projected[:, :inner_width]
    conv_in = projected[:, inner_width:inner_width + channels]
    dt_part = low_back(projected[:, inner_width + channels:])
    extended = jnp.concatenate([jnp.zeros((tap_count - 1, channels), jnp.float32), conv_in])
    ext_ids = jnp.concatenate([jnp.full((tap_count - 1,), -1, jnp.int32), doc_ids.astype(jnp.int32)])
    activated = conv_silu(extended, ext_ids, conv_weight, conv_bias)
    x_part = low_back(low(activated[:, :inner_width]))
    b_part = low(activated[:, inner_width:inner_width + state_dim])
    c_part = low(activated[:, inner_width + state_dim:])
    scanned = low_back(low(scan_heads(x_part, dt_part, b_part, c_part, doc_ids, dt_bias, a_log, skip_gain, BLOCK)))
    gated = low(gated_norm(scanned, gate_part, gate_gain))
    return residual_in + jnp.dot(gated, out_weight, precision=highest)

def reference(x_in, seg_ids, in_weight, out_weight, conv_weight, conv_bias, dt_bias, a_log, skip_gain, norm_gain, gate_gain, cotangent):
    weight_set = (in_weight.astype(jnp.float32), out_weight.astype(jnp.float32), conv_weight.astype(jnp.float32), conv_bias.astype(jnp.float32), dt_bias.astype(jnp.float32), a_log.astype(jnp.float32), skip_gain.astype(jnp.float32), norm_gain.astype(jnp.float32), gate_gain.astype(jnp.float32))
    residual_in = x_in.astype(jnp.float32)

    def forward(inputs_all, weights_all):

        def one_stream(paired):
            return jax.checkpoint(stream_forward)(paired[0], paired[1], weights_all)
        return lax.map(one_stream, (inputs_all, seg_ids))
    result, pullback = jax.vjp(forward, residual_in, weight_set)
    grad_input, grads = pullback(cotangent.astype(jnp.float32))
    return (result.astype(jnp.bfloat16), grad_input, grads[0], grads[1], grads[2], grads[3], grads[4], grads[5], grads[6], grads[7], grads[8])
```

```python
import functools

import jax
import jax.numpy as jnp
from jax import lax
from jax.experimental import pallas as pl
from jax.experimental.pallas import tpu as pltpu
from jax.sharding import PartitionSpec as P

epsilon = 1e-05
bf16, f32 = jnp.bfloat16, jnp.float32
LB = 128
GW = 256
HALO = 16
TAPS = 4
NEG = -1e30


def mm(a, b):
    return jnp.dot(a, b, preferred_element_type=f32)


def mm_nt(a, b):
    return lax.dot_general(a, b, (((1,), (1,)), ((), ())), preferred_element_type=f32)


def mm_tn(a, b):
    return lax.dot_general(a, b, (((0,), (0,)), ((), ())), preferred_element_type=f32)


def split2(v):
    hi = v.astype(bf16)
    return hi, (v - hi.astype(f32)).astype(bf16)


def split3(v):
    hi = v.astype(bf16)
    rest = v - hi.astype(f32)
    mid = rest.astype(bf16)
    return hi, mid, (rest - mid.astype(f32)).astype(bf16)


def pick(base, width, each):
    row = lax.broadcasted_iota(jnp.int32, (128, width), 0)
    col = lax.broadcasted_iota(jnp.int32, (128, width), 1) // each
    return jnp.where(row == base + col, 1.0, 0.0).astype(bf16)


def lane_sums(sel, v):
    hi, lo = split2(v)
    return mm_nt(sel, hi) + mm_nt(sel, lo)


def head_rows(hd):
    row = lax.broadcasted_iota(jnp.int32, (8, GW), 0)
    col = lax.broadcasted_iota(jnp.int32, (8, GW), 1) // hd
    return jnp.where(row == col, 1.0, 0.0).astype(bf16)


def scan_lanes(v, reverse):
    width = v.shape[1]
    lane = lax.broadcasted_iota(jnp.int32, v.shape, 1)
    s = 1
    while s < width:
        if reverse:
            v = v + jnp.where(lane < width - s, pltpu.roll(v, width - s, 1), 0.0)
        else:
            v = v + jnp.where(lane >= s, pltpu.roll(v, s, 1), 0.0)
        s *= 2
    return v


def sigmoid(v):
    return 1.0 / (1.0 + jnp.exp(-v))


def softplus(v):
    return jnp.maximum(v, 0.0) + jnp.log1p(jnp.exp(-jnp.abs(v)))


RC = 32


def fill_extended(ext, cin, rows):
    ext[0:8] = cin[rows + HALO - 8 : rows + HALO].astype(f32)
    ext[8 : 8 + rows] = cin[0:rows].astype(f32)


def conv_pre(ext, cw, masks, r):
    pre = cw[TAPS : TAPS + 1] + ext[8 + r : 8 + r + RC] * cw[TAPS - 1 : TAPS]
    for k in range(TAPS - 1):
        off = 8 - (TAPS - 1) + k + r
        pre = pre + ext[off : off + RC] * cw[k : k + 1] * masks[r : r + RC, k : k + 1]
    return pre


def kernel_a(rows, hd, cin, cw, masks, mrow, dtt, hp, xo, bco, so, cumo, stepo, colo, ext, cols, act):
    i = pl.program_id(0)
    fill_extended(ext, cin, rows)
    for r in range(0, rows, RC):
        pre = conv_pre(ext, cw, masks, r)
        act[r : r + RC] = (pre * sigmoid(pre)).astype(bf16)

    @pl.when(i == 0)
    def _():
        bco[...] = act[...]
        step = softplus(dtt[...] + hp[:, 0:1])
        cum = scan_lanes(-jnp.exp(hp[:, 1:2]) * step, False)
        stepo[...] = step
        cumo[...] = cum
        n = rows // LB
        w_in, w_end = [], []
        for c in range(n):
            own = cum[:, c * LB : (c + 1) * LB]
            if c == 0:
                w_in.append(jnp.exp(own))
            else:
                w_in.append(jnp.exp(own - cum[:, c * LB - 1 : c * LB]))
            w_end.append(jnp.exp(own[:, LB - 1 : LB] - own))
        w_in = jnp.concatenate(w_in, 1) * mrow[0:1]
        w_end = jnp.concatenate(w_end, 1) * mrow[1:2]
        w_dev = jnp.exp(cum) * mrow[2:3]
        w_all = jnp.exp(cum[:, rows - 1 : rows] - cum) * mrow[3:4] * step
        first = jnp.concatenate([cum, step], 0).T
        for q, part in enumerate(split3(first)):
            colo[q] = part
        pairs = ((w_in, w_end), (w_end * step, w_all), (w_dev, jnp.zeros_like(w_dev)))
        for q, (one, two) in enumerate(pairs):
            hi, lo = split2(jnp.concatenate([one, two], 0).T)
            colo[3 + 2 * q] = hi
            colo[4 + 2 * q] = lo
        cols[0] = colo[5]
        cols[1] = colo[6]
        cols[2] = colo[7]
        cols[3] = colo[8]
        so[...] = jnp.zeros_like(so)

    @pl.when(i > 0)
    def _():
        g = i - 1
        x = act[...]
        xo[...] = x
        sel = pick(64 + 8 * g, GW, hd)
        wexp = mm(cols[0], sel) + mm(cols[1], sel)
        xw = (x.astype(f32) * wexp).astype(bf16)
        so[0, 0:128] = mm_tn(bco[:, 0:128], xw).astype(bf16)
        sel = pick(8 * g, GW, hd)
        dev = mm(cols[2, rows - 16 : rows], sel) + mm(cols[3, rows - 16 : rows], sel)
        hi, lo = split2(dev[15:16])
        so[0, 128:144] = jnp.concatenate([hi, lo, jnp.zeros((14, GW), bf16)], 0)


def call_a(pc, cw, masks, mrow, dtt, hp, rows, di, hd):
    ng = di // GW
    nb = ng + 1
    col = lambda i: (0, (i + ng) % nb)
    grp = lambda i: (0, jnp.maximum(i - 1, 0))
    full = lambda i: (0, 0)
    return pl.pallas_call(
        functools.partial(kernel_a, rows, hd),
        grid=(nb,),
        in_specs=[
            pl.BlockSpec((rows + HALO, GW), col),
            pl.BlockSpec((8, GW), col),
            pl.BlockSpec((rows, 8), full),
            pl.BlockSpec((8, rows), full),
            pl.BlockSpec((64, rows), full),
            pl.BlockSpec((64, 8), full),
        ],
        out_specs=[
            pl.BlockSpec((rows, GW), grp),
            pl.BlockSpec((rows, GW), full),
            pl.BlockSpec((1, 144, GW), lambda i: (jnp.maximum(i - 1, 0), 0, 0)),
            pl.BlockSpec((64, rows), full),
            pl.BlockSpec((64, rows), full),
            pl.BlockSpec((9, rows, 128), lambda i: (0, 0, 0)),
        ],
        out_shape=[
            jax.ShapeDtypeStruct((rows, di), bf16),
            jax.ShapeDtypeStruct((rows, GW), bf16),
            jax.ShapeDtypeStruct((ng, 144, GW), bf16),
            jax.ShapeDtypeStruct((64, rows), f32),
            jax.ShapeDtypeStruct((64, rows), f32),
            jax.ShapeDtypeStruct((9, rows, 128), bf16),
        ],
        scratch_shapes=[
            pltpu.VMEM((rows + 8, GW), f32),
            pltpu.VMEM((4, rows, 128), bf16),
            pltpu.VMEM((rows, GW), bf16),
        ],
        compiler_params=pltpu.CompilerParams(dimension_semantics=("arbitrary",)),
        cost_estimate=pl.CostEstimate(flops=400000000, bytes_accessed=6000000, transcendentals=2400000),
        name="conv_state",
    )(pc, cw, masks, mrow, dtt, hp)


def kernel_f(n, recv, sin, dec):
    state = jnp.zeros((128, GW), f32)
    for i in range(n):
        sin[i] = state.astype(bf16)
        d = recv[i, 128:129].astype(f32) + recv[i, 129:130].astype(f32)
        dec[i] = jnp.broadcast_to(d, (8, GW))
        state = state * d + recv[i, 0:128].astype(f32)


def call_f(recv):
    n = recv.shape[0]
    return pl.pallas_call(
        functools.partial(kernel_f, n),
        out_shape=[
            jax.ShapeDtypeStruct((n, 128, GW), bf16),
            jax.ShapeDtypeStruct((n, 8, GW), f32),
        ],
        name="join_forward",
    )(recv)


def kernel_g(n, recv, dec, gin):
    adj = jnp.zeros((128, GW), f32)
    for i in reversed(range(n)):
        gin[i] = adj.astype(bf16)
        adj = adj * dec[i, 0:1] + recv[i].astype(f32)


def call_g(recv, dec):
    n = recv.shape[0]
    return pl.pallas_call(
        functools.partial(kernel_g, n),
        out_shape=jax.ShapeDtypeStruct((n, 128, GW), bf16),
        name="join_backward",
    )(recv, dec)


def negmask(masks, mrow, c, flip):
    rows = slice(c * LB, (c + 1) * LB)
    same = masks[rows, 3:4] == mrow[4:5, rows]
    a = lax.broadcasted_iota(jnp.int32, (LB, LB), 0)
    b = lax.broadcasted_iota(jnp.int32, (LB, LB), 1)
    order = (a <= b) if flip else (b <= a)
    return jnp.where(same & order, 0.0, NEG)


def half_masks(hd):
    lane = lax.broadcasted_iota(jnp.int32, (LB, 128), 1)
    low = jnp.where(lane < hd, 1.0, 0.0).astype(bf16)
    high = jnp.where(lane < hd, 0.0, 1.0).astype(bf16)
    return low, high


def kernel_b(rows, hd, g0, x, bc, cols, cumt, stept, masks, mrow, yo, score, neg, cumb, st):
    i = pl.program_id(0)
    g = g0 + i
    n = rows // LB

    @pl.when(i == 0)
    def _():
        for c in range(n):
            r = slice(c * LB, (c + 1) * LB)
            score[c] = mm_nt(bc[r, 128:256], bc[r, 0:128])
            neg[c] = negmask(masks, mrow, c, False)

    sel = pick(8 * g, 4 * LB, LB)
    cumb[...] = mm(cols[0], sel) + mm(cols[1], sel) + mm(cols[2], sel)
    sel = pick(8 * g, GW, hd)
    low, high = half_masks(hd)
    for c in range(n):
        r = slice(c * LB, (c + 1) * LB)
        outs = []
        for p in range(2):
            mats = []
            for j in range(2):
                h = 2 * p + j
                diff = cumb[r, h * LB : (h + 1) * LB] - cumt[h : h + 1, r]
                m = jnp.exp(diff + neg[c]) * score[c] * stept[h : h + 1, r]
                mats.append(m.astype(bf16))
            xp = x[r, 128 * p : 128 * (p + 1)]
            outs.append(mm(jnp.concatenate(mats, 1), jnp.concatenate([xp * low, xp * high], 0)))
        y = jnp.concatenate(outs, 1)
        if c > 0:
            w_in = mm(cols[3, r], sel) + mm(cols[4, r], sel)
            y = y + mm(bc[r, 128:256], st[...].astype(bf16)) * w_in
        yo[r] = y
        if c < n - 1:
            w_end = mm(cols[5, r], sel) + mm(cols[6, r], sel)
            fresh = mm_tn(bc[r, 0:128], (x[r].astype(f32) * w_end).astype(bf16))
            if c > 0:
                fresh = fresh + st[...] * w_in[LB - 1 : LB]
            st[...] = fresh


def call_b(x, bc, cols, cumt, stept, masks, mrow, rows, hd, g0, count):
    n = rows // LB
    grp = lambda i: (0, g0 + i)
    row = lambda i: (g0 + i, 0)
    full = lambda i: (0, 0)
    return pl.pallas_call(
        functools.partial(kernel_b, rows, hd, g0),
        grid=(count,),
        in_specs=[
            pl.BlockSpec((rows, GW), grp),
            pl.BlockSpec((rows, GW), full),
            pl.BlockSpec((9, rows, 128), lambda i: (0, 0, 0)),
            pl.BlockSpec((8, rows), row),
            pl.BlockSpec((8, rows), row),
            pl.BlockSpec((rows, 8), full),
            pl.BlockSpec((8, rows), full),
        ],
        out_specs=pl.BlockSpec((rows, GW), lambda i: (0, i)),
        out_shape=jax.ShapeDtypeStruct((rows, count * GW), f32),
        scratch_shapes=[
            pltpu.VMEM((n, LB, LB), f32),
            pltpu.VMEM((n, LB, LB), f32),
            pltpu.VMEM((rows, 4 * LB), f32),
            pltpu.VMEM((128, GW), f32),
        ],
        compiler_params=pltpu.CompilerParams(dimension_semantics=("arbitrary",)),
        cost_estimate=pl.CostEstimate(flops=800000000, bytes_accessed=4000000, transcendentals=1000000),
        name="scan_forward",
    )(x, bc, cols, cumt, stept, masks, mrow)


SR = 16


def kernel_c(ng, hd, ya, yb, x, bc, sin, cols, gate, gg, skip, gain, gated, gscan, ggate, ggain, go, sel, ys, ws, gw, acc):
    i = pl.program_id(0)
    half = ya.shape[1]
    di = 2 * half

    @pl.when(i == 0)
    def _():
        for g in range(ng):
            sel[:, g * GW : (g + 1) * GW] = pick(8 * g, GW, hd)
        ggain[...] = jnp.zeros_like(ggain)
        acc[...] = jnp.zeros_like(acc)

    for g in range(ng):
        k = slice(g * GW, (g + 1) * GW)
        w = mm(cols[0], sel[:, k]) + mm(cols[1], sel[:, k])
        ws[:, k] = w
        ys[:, k] = mm(bc[:, 128:256], sin[g]) * w
    inv_di = 1.0 / di

    def body(q, carry):
        r = pl.ds(pl.multiple_of(q * SR, SR), SR)
        local = jnp.concatenate([ya[r, :], yb[r, :]], 1)
        y = local + ys[r, :] + skip[0:1] * x[r, :].astype(f32)
        scanned = y.astype(bf16).astype(f32)
        gt = gate[r, :].astype(f32)
        sg = sigmoid(gt)
        sil = gt * sg
        v = scanned * sil
        ginv = lax.rsqrt(jnp.sum(v * v, 1, keepdims=True) * inv_di + epsilon)
        vn = v * ginv
        gated[r, :] = (vn * gain[0:1]).astype(bf16)
        grad = gg[r, :]
        part = grad * vn
        ggain[0:8] += part[0:8] + part[8:16]
        gl = gain[0:1] * grad
        mean = jnp.sum(gl * v, 1, keepdims=True) * inv_di
        gv = ginv * (gl - v * (ginv * ginv * mean))
        gs = (gv * sil).astype(bf16)
        gscan[r, :] = gs
        ggate[r, :] = (gv * scanned * (sg * (1.0 + gt * (1.0 - sg)))).astype(bf16)
        gw[r, :] = (gs.astype(f32) * ws[r, :]).astype(bf16)
        return carry

    lax.fori_loop(0, LB // SR, body, 0)
    for g in range(ng):
        k = slice(g * GW, (g + 1) * GW)
        acc[g] += mm_tn(bc[:, 128:256], gw[:, k])

    @pl.when(i == pl.num_programs(0) - 1)
    def _():
        go[...] = acc[...].astype(bf16)


def call_c(ya, yb, x, bc, sin, cols, gate, gg, skip, gain, rows, di, hd):
    ng = di // GW
    row = lambda i: (i, 0)
    full = lambda i: (0, 0)
    cube = lambda i: (0, 0, 0)
    wide = pl.BlockSpec((LB, di), row)
    return pl.pallas_call(
        functools.partial(kernel_c, ng, hd),
        grid=(rows // LB,),
        in_specs=[
            pl.BlockSpec((LB, di // 2), row),
            pl.BlockSpec((LB, di // 2), row),
            wide,
            pl.BlockSpec((LB, GW), row),
            pl.BlockSpec((ng, 128, GW), cube),
            pl.BlockSpec((2, LB, 128), lambda i: (0, i, 0)),
            wide,
            wide,
            pl.BlockSpec((8, di), full),
            pl.BlockSpec((8, di), full),
        ],
        out_specs=[wide, wide, wide, pl.BlockSpec((8, di), full), pl.BlockSpec((ng, 128, GW), cube)],
        out_shape=[
            jax.ShapeDtypeStruct((rows, di), bf16),
            jax.ShapeDtypeStruct((rows, di), bf16),
            jax.ShapeDtypeStruct((rows, di), bf16),
            jax.ShapeDtypeStruct((8, di), f32),
            jax.ShapeDtypeStruct((ng, 128, GW), bf16),
        ],
        scratch_shapes=[
            pltpu.VMEM((128, di), bf16),
            pltpu.VMEM((LB, di), f32),
            pltpu.VMEM((LB, di), f32),
            pltpu.VMEM((LB, di), bf16),
            pltpu.VMEM((ng, 128, GW), f32),
        ],
        compiler_params=pltpu.CompilerParams(dimension_semantics=("arbitrary",)),
        cost_estimate=pl.CostEstimate(flops=1200000000, bytes_accessed=20000000, transcendentals=2000000),
        name="gate_both",
    )(ya, yb, x, bc, sin, cols, gate, gg, skip, gain)


def kernel_d(rows, hd, x, dy, bc, cols, cumt, stept, stepall, masks, mrow, sin, gin, cin, cw, skip, dtt, hp,
             gci, tail, rim, gcw, gdt, hsum,
             score, neg, cumb, stepb, states, zsum, gact, dbc, ext, shifted, arow, crow, grow, xrow, adj):
    i = pl.program_id(0)
    n = rows // LB
    last = pl.num_programs(0) - 1

    @pl.when(i == 0)
    def _():
        for c in range(n):
            r = slice(c * LB, (c + 1) * LB)
            score[c] = mm_nt(bc[r, 0:128], bc[r, 128:256])
            neg[c] = negmask(masks, mrow, c, True)
        zsum[...] = jnp.zeros_like(zsum)
        dbc[...] = jnp.zeros_like(dbc)
        zero = jnp.zeros((8, GW), f32)
        for k in range(TAPS):
            shifted[k, 0:8] = zero
            shifted[k, rows + 8 : rows + 16] = zero

    @pl.when(i < last)
    def _():
        g = i
        sel = pick(8 * g, 4 * LB, LB)
        cumb[...] = mm(cols[0], sel) + mm(cols[1], sel) + mm(cols[2], sel)
        sel = pick(64 + 8 * g, 4 * LB, LB)
        stepb[...] = mm(cols[0], sel) + mm(cols[1], sel) + mm(cols[2], sel)
        sel0 = pick(8 * g, GW, hd)
        sel64 = pick(64 + 8 * g, GW, hd)
        heads = head_rows(hd)
        low, high = half_masks(hd)
        lane = lax.broadcasted_iota(jnp.int32, (LB, 128), 1)
        states[0] = sin[0]
        run = sin[0].astype(f32)
        for c in range(n - 1):
            r = slice(c * LB, (c + 1) * LB)
            e = slice((c + 1) * LB - 16, (c + 1) * LB)
            dec = (mm(cols[3, e], sel0) + mm(cols[4, e], sel0))[15:16]
            w_es = mm(cols[5, r], sel0) + mm(cols[6, r], sel0)
            run = run * dec + mm_tn(bc[r, 0:128], (x[r].astype(f32) * w_es).astype(bf16))
            states[c + 1] = run.astype(bf16)
        adj[...] = gin[0].astype(f32)
        slot = pl.ds(pl.multiple_of(8 * g, 8), 8)
        skipsum = jnp.zeros((1, GW), f32)
        for c in reversed(range(n)):
            r = slice(c * LB, (c + 1) * LB)
            xf = x[r].astype(f32)
            dyf = dy[r].astype(f32)
            b_c, c_c = bc[r, 0:128], bc[r, 128:256]
            w_in = mm(cols[3, r], sel0) + mm(cols[4, r], sel0)
            w_end = mm(cols[3, r], sel64) + mm(cols[4, r], sel64)
            w_es = mm(cols[5, r], sel0) + mm(cols[6, r], sel0)
            st_e = mm(cols[0, r], sel64) + mm(cols[1, r], sel64)
            big = adj[...]
            adj_b = big.astype(bf16)
            st_b = states[c]
            du_out = mm(b_c, adj_b) * w_end
            dbc[r, 0:128] += mm_nt((xf * w_es).astype(bf16), adj_b)
            dyw = dyf * w_in
            dyw_b = dyw.astype(bf16)
            dbc[r, 128:256] += mm_nt(dyw_b, st_b)
            from_state = lane_sums(heads, dyw * mm(c_c, st_b))
            dec = w_in[LB - 1 : LB]
            cross = jnp.sum(big * st_b.astype(f32), 0, keepdims=True) * dec
            cross = lane_sums(heads, jnp.broadcast_to(cross, (LB, GW)))
            adj[...] = big * dec + mm_tn(c_c, dyw_b)
            x_out = lane_sums(heads, xf * du_out)
            zacc = zsum[c]
            pcol = jnp.zeros((LB, 128), f32)
            rsum = []
            dus = []
            for p in range(2):
                k = slice(128 * p, 128 * (p + 1))
                xp, dyp = x[r, k], dy[r, k]
                both = mm_nt(jnp.concatenate([xp * low, xp * high], 0), dyp)
                mats = []
                for j in range(2):
                    h = 2 * p + j
                    hb = slice(h * LB, (h + 1) * LB)
                    diff = cumt[h : h + 1, r] - cumb[r, hb]
                    dmat = jnp.exp(diff + neg[c])
                    kmat = dmat * both[j * LB : (j + 1) * LB]
                    kq = kmat * score[c]
                    sb = stepb[r, hb]
                    zacc = zacc + kmat * sb
                    pcol = jnp.where(lane == h, jnp.sum(kq, 1, keepdims=True), pcol)
                    rsum.append(jnp.sum(kq * sb, 0, keepdims=True))
                    mats.append((dmat * score[c]).astype(bf16))
                dus.append(mm(jnp.concatenate(mats, 1), jnp.concatenate([dyp * low, dyp * high], 0)))
            zsum[c] = zacc
            p_t = pcol.T[0:8]
            rsum = jnp.concatenate(rsum + [jnp.zeros((4, LB), f32)], 0)
            arow[slot, r] = rsum - stept[:, r] * p_t + from_state
            crow[slot, r] = stept[:, r] * x_out
            grow[slot, r] = cross
            xrow[slot, r] = p_t + x_out
            du = jnp.concatenate(dus, 1) + du_out
            gx = st_e * du + skip[0:1] * dyf
            gact[r] = gx.astype(bf16).astype(f32)
            skipsum = skipsum + jnp.sum(xf * dyf, 0, keepdims=True)
        gcw[TAPS + 1 : TAPS + 2] = skipsum

    @pl.when(i == last)
    def _():
        for c in range(n):
            r = slice(c * LB, (c + 1) * LB)
            z = zsum[c].astype(bf16)
            gact[r, 0:128] = dbc[r, 0:128] + mm(z, bc[r, 128:256])
            gact[r, 128:256] = dbc[r, 128:256] + mm_tn(z, bc[r, 0:128])
        rate = jnp.exp(hp[:, 1:2])
        sums = jnp.zeros((64, 1), f32)
        alog = jnp.zeros((64, 1), f32)
        for c in range(n):
            r = slice(c * LB, (c + 1) * LB)
            cr = crow[:, r]
            gl = scan_lanes(arow[:, r], True) + scan_lanes(cr, False) - cr + grow[:, r]
            grad = (xrow[:, r] - rate * gl) * sigmoid(dtt[:, r] + hp[:, 0:1])
            gdt[:, r] = grad
            sums = sums + jnp.sum(grad, 1, keepdims=True)
            alog = alog - jnp.sum(gl * (rate * stepall[:, r]), 1, keepdims=True)
        lane = lax.broadcasted_iota(jnp.int32, (64, 128), 1)
        hsum[...] = jnp.where(lane == 0, sums, jnp.where(lane == 1, alog, 0.0))
        gcw[TAPS + 1 : TAPS + 2] = jnp.zeros((1, GW), f32)

    fill_extended(ext, cin, rows)
    parts = [jnp.zeros((8, GW), f32) for _ in range(TAPS + 1)]
    for r in range(0, rows, RC):
        pre = conv_pre(ext, cw, masks, r)
        s = sigmoid(pre)
        gp = gact[r : r + RC] * (s * (1.0 + pre * (1.0 - s)))
        for k in range(TAPS):
            gm = gp if k == TAPS - 1 else gp * masks[r : r + RC, k : k + 1]
            shifted[k, 8 + r : 8 + r + RC] = gm
            off = 8 - (TAPS - 1) + k + r
            prod = gm * ext[off : off + RC]
            for q in range(0, RC, 8):
                parts[k] = parts[k] + prod[q : q + 8]
        for q in range(0, RC, 8):
            parts[TAPS] = parts[TAPS] + gp[q : q + 8]
    for k in range(TAPS + 1):
        gcw[k : k + 1] = jnp.sum(parts[k], 0, keepdims=True)

    def back(start, count):
        total = None
        for k in range(TAPS):
            off = start + TAPS - 1 - k
            term = shifted[k, off : off + count] * cw[k : k + 1]
            total = term if total is None else total + term
        return total

    rim[...] = back(0, 8)
    for r in range(0, rows, RC):
        value = back(8 + r, RC)
        gci[r : r + RC] = value.astype(bf16)
        if r == rows - RC:
            tail[...] = value[RC - HALO : RC]


def call_d(x, dy, bc, cols, cumt, stept, masks, mrow, sin, gin, pc, cw, skip, dtt, hp, rows, di, hd):
    ng = di // GW
    n = rows // LB
    ch = di + GW
    own = lambda i: (0, jnp.minimum(i, ng - 1))
    row = lambda i: (jnp.minimum(i, ng - 1), 0)
    cube = lambda i: (jnp.minimum(i, ng - 1), 0, 0)
    blk = lambda i: (0, i)
    full = lambda i: (0, 0)
    return pl.pallas_call(
        functools.partial(kernel_d, rows, hd),
        grid=(ng + 1,),
        in_specs=[
            pl.BlockSpec((rows, GW), own),
            pl.BlockSpec((rows, GW), own),
            pl.BlockSpec((rows, GW), full),
            pl.BlockSpec((9, rows, 128), lambda i: (0, 0, 0)),
            pl.BlockSpec((8, rows), row),
            pl.BlockSpec((8, rows), row),
            pl.BlockSpec((64, rows), full),
            pl.BlockSpec((rows, 8), full),
            pl.BlockSpec((8, rows), full),
            pl.BlockSpec((1, 128, GW), cube),
            pl.BlockSpec((1, 128, GW), cube),
            pl.BlockSpec((rows + HALO, GW), blk),
            pl.BlockSpec((8, GW), blk),
            pl.BlockSpec((8, GW), own),
            pl.BlockSpec((64, rows), full),
            pl.BlockSpec((64, 8), full),
        ],
        out_specs=[
            pl.BlockSpec((rows, GW), blk),
            pl.BlockSpec((HALO, GW), blk),
            pl.BlockSpec((8, GW), blk),
            pl.BlockSpec((8, GW), blk),
            pl.BlockSpec((64, rows), full),
            pl.BlockSpec((64, 128), full),
        ],
        out_shape=[
            jax.ShapeDtypeStruct((rows, ch), bf16),
            jax.ShapeDtypeStruct((HALO, ch), f32),
            jax.ShapeDtypeStruct((8, ch), f32),
            jax.ShapeDtypeStruct((8, ch), f32),
            jax.ShapeDtypeStruct((64, rows), f32),
            jax.ShapeDtypeStruct((64, 128), f32),
        ],
        scratch_shapes=[
            pltpu.VMEM((n, LB, LB), f32),
            pltpu.VMEM((n, LB, LB), f32),
            pltpu.VMEM((rows, 4 * LB), f32),
            pltpu.VMEM((rows, 4 * LB), f32),
            pltpu.VMEM((n, 128, GW), bf16),
            pltpu.VMEM((n, LB, LB), f32),
            pltpu.VMEM((rows, GW), f32),
            pltpu.VMEM((rows, GW), f32),
            pltpu.VMEM((rows + 8, GW), f32),
            pltpu.VMEM((TAPS, rows + 16, GW), f32),
            pltpu.VMEM((64, rows), f32),
            pltpu.VMEM((64, rows), f32),
            pltpu.VMEM((64, rows), f32),
            pltpu.VMEM((64, rows), f32),
            pltpu.VMEM((128, GW), f32),
        ],
        compiler_params=pltpu.CompilerParams(dimension_semantics=("arbitrary",)),
        cost_estimate=pl.CostEstimate(flops=4000000000, bytes_accessed=14000000, transcendentals=4000000),
        name="scan_backward",
    )(x, dy, bc, cols, cumt, stept, stept, masks, mrow, sin, gin, pc, cw, skip, dtt, hp)


def slots(values, per):
    groups = values.shape[0] // per
    shaped = values.reshape((groups, per) + values.shape[1:])
    pad = [(0, 0), (0, 8 - per)] + [(0, 0)] * (values.ndim - 1)
    return jnp.pad(shaped, pad).reshape((groups * 8,) + values.shape[1:])


def unslots(values, per):
    groups = values.shape[0] // 8
    return values.reshape((groups, 8) + values.shape[1:])[:, :per].reshape((groups * per,) + values.shape[1:])


def gather_small(value, axis):
    count = lax.axis_size(axis)
    wide = jnp.broadcast_to(value[None], (count,) + value.shape)
    return lax.all_to_all(wide, axis, split_axis=0, concat_axis=0, tiled=True)


def gather_weight(shard):
    part = shard.shape[0] // lax.axis_size("seq")
    mine = lax.dynamic_slice_in_dim(shard, lax.axis_index("seq") * part, part)
    return lax.all_gather(mine, ("wsh", "seq"), axis=0, tiled=True)


def reduce_weight(grad):
    part = lax.psum_scatter(grad, "seq", scatter_dimension=0, tiled=True)
    part = lax.psum_scatter(part, "wsh", scatter_dimension=0, tiled=True)
    return lax.all_gather(part, "seq", axis=0, tiled=True)


def local(x_in, seg_ids, in_weight, out_weight, conv_weight, conv_bias, dt_bias, a_log, skip_gain, norm_gain, gate_gain, cotangent):
    nseq, nw = lax.axis_size("seq"), lax.axis_size("wsh")
    me = lax.axis_index("seq")
    rows, d = x_in.shape[1:]
    e = in_weight.shape[1]
    di = out_weight.shape[0] * nw
    heads = dt_bias.shape[0] * nw
    ch = conv_bias.shape[0] * nw
    hd = di // heads
    per = GW // hd
    ng = di // GW
    x, ids, cot = x_in[0], seg_ids[0], cotangent[0]

    forward = [(i, i + 1) for i in range(nseq - 1)]
    x_halo = lax.ppermute(x[rows - HALO :], "seq", forward)
    id_halo = lax.ppermute(ids[rows - HALO :], "seq", forward)
    id_halo = jnp.where(me == 0, -1, id_halo)

    w_cd = gather_weight(in_weight[:, di:])
    w_gate = gather_weight(in_weight[:, :di])
    w_out = gather_weight(out_weight)
    small = [conv_weight.reshape(-1), conv_bias, dt_bias, a_log, skip_gain, norm_gain, gate_gain]
    sizes = [s.shape[0] for s in small]
    packed = gather_small(jnp.concatenate(small), "wsh")
    cut, at = [], 0
    for s in sizes:
        cut.append(packed[:, at : at + s].astype(f32))
        at += s
    conv_w = cut[0].reshape(nw, TAPS, -1).transpose(1, 0, 2).reshape(TAPS, ch)
    conv_b, dtb, alog, skip_g, norm_g, gate_g = [c.reshape(-1) for c in cut[1:]]
    cw = jnp.concatenate([conv_w, conv_b[None], jnp.zeros((3, ch), f32)], 0)
    hp = jnp.pad(jnp.stack([slots(dtb, per), slots(alog, per)], 1), ((0, 0), (0, 6)))
    skip = jnp.broadcast_to(jnp.repeat(skip_g, hd)[None], (8, di))
    gain = jnp.broadcast_to(gate_g[None], (8, di))

    ext_ids = jnp.concatenate([id_halo[HALO - 3 :], ids])
    prev = id_halo[HALO - 1]
    before = jnp.repeat(jnp.concatenate([prev[None], ids[LB - 1 :: LB][:-1]]), LB)
    ends = jnp.repeat(ids[LB - 1 :: LB], LB)
    zero = jnp.zeros((rows,), f32)
    masks = jnp.stack([(ext_ids[k : k + rows] == ids).astype(f32) for k in range(3)] + [ids.astype(f32)] + [zero] * 4, 1)
    mrow = jnp.stack(
        [(ids == before).astype(f32), (ids == ends).astype(f32), (ids == prev).astype(f32), (ids == ids[rows - 1]).astype(f32), ids.astype(f32)]
        + [zero] * 3,
        0,
    )

    xf = jnp.concatenate([x, x_halo], 0).astype(f32)
    rinv = lax.rsqrt(jnp.mean(xf * xf, 1, keepdims=True) + epsilon)
    normed = (xf * rinv * norm_g[None]).astype(bf16)
    pc = mm(normed, w_cd).astype(bf16)
    normed_own = normed[:rows]
    dtt = slots(pc[:rows, ch:].T.astype(f32), per)

    xp, bc, s_loc, cumt, stept, cols = call_a(pc, cw, masks, mrow, dtt, hp, rows, di, hd)
    recv = lax.all_to_all(s_loc, "seq", split_axis=0, concat_axis=0, tiled=True)
    ya = call_b(xp, bc, cols, cumt, stept, masks, mrow, rows, hd, 0, ng // 2)
    s_all, dec = call_f(recv)
    s_in = lax.all_to_all(s_all, "seq", split_axis=0, concat_axis=0, tiled=True)
    yb = call_b(xp, bc, cols, cumt, stept, masks, mrow, rows, hd, ng // 2, ng - ng // 2)

    gate = mm(normed_own, w_gate).astype(bf16)
    gg = mm_nt(cot, w_out)
    gated, gscan, ggate, ggain, g_loc = call_c(ya, yb, xp, bc, s_in, cols[7:9], gate, gg, skip, gain, rows, di, hd)
    g_recv = lax.all_to_all(g_loc, "seq", split_axis=0, concat_axis=0, tiled=True)
    g_all = call_g(g_recv, dec)
    g_in = lax.all_to_all(g_all, "seq", split_axis=0, concat_axis=0, tiled=True)

    output = (x.astype(f32) + mm(gated, w_out)).astype(bf16)

    def ordered(values):
        r = values.shape[0] // (nw * nseq)
        return values.reshape(nw, nseq, r, values.shape[1]).transpose(1, 0, 2, 3).reshape(values.shape)

    r = d // (nw * nseq)
    normed_t = normed_own.reshape(rows, nw, nseq, r).transpose(0, 2, 1, 3).reshape(rows, d)
    grad_wout = reduce_weight(ordered(mm_tn(gated, cot).astype(bf16)))
    grad_wgate = reduce_weight(mm_tn(normed_t, ggate).astype(bf16))
    gn_gate = mm_nt(ggate, w_gate)

    gci, tail, rim, gcw, gdt, hsum = call_d(
        xp, gscan, bc, cols, cumt, stept, masks, mrow, s_in, g_in, pc, cw, skip, dtt, hp, rows, di, hd
    )
    backward = [(i + 1, i) for i in range(nseq - 1)]
    rim_next = lax.ppermute(rim[8 - (TAPS - 1) :], "seq", backward)
    fixed = jnp.concatenate([tail[: HALO - (TAPS - 1)], tail[HALO - (TAPS - 1) :] + rim_next], 0)
    gci = lax.dynamic_update_slice(gci, fixed.astype(bf16), (rows - HALO, 0))
    gcd = jnp.concatenate([gci, unslots(gdt, per).T.astype(bf16)], 1)
    grad_wcd = reduce_weight(mm_tn(normed_t, gcd).astype(bf16))
    gnorm = gn_gate + mm_nt(gcd, w_cd)
    x_own, rinv_own = xf[:rows], rinv[:rows]
    grad_norm = jnp.sum(gnorm * x_own * rinv_own, 0)
    gl = gnorm * norm_g[None]
    mean = jnp.mean(gl * x_own, 1, keepdims=True)
    grad_input = cot.astype(f32) + rinv_own * (gl - x_own * (rinv_own * rinv_own * mean))

    pieces = [
        gcw[:TAPS].reshape(TAPS, nw, -1).transpose(1, 0, 2).reshape(nw, -1),
        gcw[TAPS].reshape(nw, -1),
        unslots(hsum[:, 0], per).reshape(nw, -1),
        unslots(hsum[:, 1], per).reshape(nw, -1),
        jnp.sum(gcw[TAPS + 1, :di].reshape(heads, hd), 1).reshape(nw, -1),
        grad_norm.reshape(nw, -1),
        jnp.sum(ggain, 0).reshape(nw, -1),
    ]
    stacked = lax.all_to_all(jnp.concatenate(pieces, 1), "wsh", split_axis=0, concat_axis=0, tiled=True)
    total = jnp.sum(gather_small(jnp.sum(stacked, 0), "seq"), 0)
    outs, at = [], 0
    for s in sizes:
        outs.append(total[at : at + s])
        at += s
    return (
        output[None],
        grad_input[None],
        jnp.concatenate([grad_wgate, grad_wcd], 1).astype(f32),
        grad_wout.astype(f32),
        outs[0].reshape(TAPS, -1),
        outs[1],
        outs[2],
        outs[3],
        outs[4],
        outs[5],
        outs[6],
    )


def solution(mesh):
    act, wide, vec = P("wsh", "seq", None), P("wsh", None), P("wsh")
    in_specs = (act, P("wsh", "seq"), wide, wide, P(None, "wsh"), vec, vec, vec, vec, vec, vec, act)
    out_specs = (act, act, wide, wide, P(None, "wsh"), vec, vec, vec, vec, vec, vec)
    return jax.shard_map(local, mesh=mesh, in_specs=in_specs, out_specs=out_specs, check_vma=False)
```

```python
import functools

import jax
import jax.numpy as jnp
from jax import lax
from jax.experimental import pallas as pl
from jax.experimental.pallas import tpu as pltpu
from jax.sharding import PartitionSpec as P

epsilon = 1e-05
bf16, f32 = jnp.bfloat16, jnp.float32
LB = 128
GW = 256
HALO = 16
TAPS = 4
NEG = -1e30


def mm(a, b):
    return jnp.dot(a, b, preferred_element_type=f32)


def mm_nt(a, b):
    return lax.dot_general(a, b, (((1,), (1,)), ((), ())), preferred_element_type=f32)


def mm_tn(a, b):
    return lax.dot_general(a, b, (((0,), (0,)), ((), ())), preferred_element_type=f32)


def split2(v):
    hi = v.astype(bf16)
    return hi, (v - hi.astype(f32)).astype(bf16)


def split3(v):
    hi = v.astype(bf16)
    rest = v - hi.astype(f32)
    mid = rest.astype(bf16)
    return hi, mid, (rest - mid.astype(f32)).astype(bf16)


def pick(base, width, each):
    row = lax.broadcasted_iota(jnp.int32, (128, width), 0)
    col = lax.broadcasted_iota(jnp.int32, (128, width), 1) // each
    return jnp.where(row == base + col, 1.0, 0.0).astype(bf16)


def lane_sums(sel, v):
    hi, lo = split2(v)
    return mm_nt(sel, hi) + mm_nt(sel, lo)


def head_rows(hd):
    row = lax.broadcasted_iota(jnp.int32, (8, GW), 0)
    col = lax.broadcasted_iota(jnp.int32, (8, GW), 1) // hd
    return jnp.where(row == col, 1.0, 0.0).astype(bf16)


def scan_lanes(v, reverse):
    width = v.shape[1]
    lane = lax.broadcasted_iota(jnp.int32, v.shape, 1)
    s = 1
    while s < width:
        if reverse:
            v = v + jnp.where(lane < width - s, pltpu.roll(v, width - s, 1), 0.0)
        else:
            v = v + jnp.where(lane >= s, pltpu.roll(v, s, 1), 0.0)
        s *= 2
    return v


def sigmoid(v):
    return 1.0 / (1.0 + jnp.exp(-v))


def softplus(v):
    return jnp.maximum(v, 0.0) + jnp.log1p(jnp.exp(-jnp.abs(v)))


RC = 32


def fill_extended(ext, cin, rows):
    ext[0:8] = cin[rows + HALO - 8 : rows + HALO].astype(f32)
    ext[8 : 8 + rows] = cin[0:rows].astype(f32)


def conv_pre(ext, cw, masks, r):
    pre = cw[TAPS : TAPS + 1] + ext[8 + r : 8 + r + RC] * cw[TAPS - 1 : TAPS]
    for k in range(TAPS - 1):
        off = 8 - (TAPS - 1) + k + r
        pre = pre + ext[off : off + RC] * cw[k : k + 1] * masks[r : r + RC, k : k + 1]
    return pre


def flat(w):
    return w.reshape(w.shape[0] * w.shape[1], w.shape[2])


def kernel_a(rows, hd, per, nq, me, nm, wx, wy, wb, cw, masks, mrow, hp, pxo, xo, bco, so, cumo, stepo, dto, colo, ext, cols, act):
    i = pl.program_id(0)

    @pl.when(i == 0)
    def _():
        w = wb[...].reshape(wb.shape[0] * wb.shape[1], wb.shape[2])
        out = mm(nm[...], w).astype(bf16)
        pxo[...] = out[:, 0:GW]
        dt = out[0:rows, GW : GW + 128].astype(f32).T
        pieces = []
        for g in range(8):
            pieces += [dt[per * g : per * (g + 1)], jnp.zeros((8 - per, rows), f32)]
        dto[...] = jnp.concatenate(pieces, 0)

    @pl.when((i > 0) & (i <= nq))
    def _():
        pxo[...] = mm(nm[...], flat(wx[0])).astype(bf16)

    @pl.when(i > nq)
    def _():
        pxo[...] = mm(nm[...], flat(wy[0])).astype(bf16)

    fill_extended(ext, pxo, rows)
    for r in range(0, rows, RC):
        pre = conv_pre(ext, cw, masks, r)
        act[r : r + RC] = (pre * sigmoid(pre)).astype(bf16)

    @pl.when(i == 0)
    def _():
        bco[...] = act[...]
        step = softplus(dto[...] + hp[:, 0:1])
        cum = scan_lanes(-jnp.exp(hp[:, 1:2]) * step, False)
        stepo[...] = step
        cumo[...] = cum
        n = rows // LB
        w_in, w_end = [], []
        for c in range(n):
            own = cum[:, c * LB : (c + 1) * LB]
            if c == 0:
                w_in.append(jnp.exp(own))
            else:
                w_in.append(jnp.exp(own - cum[:, c * LB - 1 : c * LB]))
            w_end.append(jnp.exp(own[:, LB - 1 : LB] - own))
        w_in = jnp.concatenate(w_in, 1) * mrow[0:1]
        w_end = jnp.concatenate(w_end, 1) * mrow[1:2]
        w_dev = jnp.exp(cum) * mrow[2:3]
        w_all = jnp.exp(cum[:, rows - 1 : rows] - cum) * mrow[3:4] * step
        first = jnp.concatenate([cum, step], 0).T
        for q, part in enumerate(split3(first)):
            colo[q] = part
        pairs = ((w_in, w_end), (w_end * step, w_all), (w_dev, jnp.zeros_like(w_dev)))
        for q, (one, two) in enumerate(pairs):
            hi, lo = split2(jnp.concatenate([one, two], 0).T)
            colo[3 + 2 * q] = hi
            colo[4 + 2 * q] = lo
        cols[0] = colo[5]
        cols[1] = colo[6]
        cols[2] = colo[7]
        cols[3] = colo[8]
        so[...] = jnp.zeros_like(so)

    @pl.when(i > 0)
    def _():
        g = block_of(i - 1, me, nq)
        x = act[...]
        xo[...] = x
        sel = pick(64 + 8 * g, GW, hd)
        wexp = mm(cols[0], sel) + mm(cols[1], sel)
        xw = (x.astype(f32) * wexp).astype(bf16)
        so[0, 0:128] = mm_tn(bco[:, 0:128], xw).astype(bf16)
        sel = pick(8 * g, GW, hd)
        dev = mm(cols[2, rows - 16 : rows], sel) + mm(cols[3, rows - 16 : rows], sel)
        hi, lo = split2(dev[15:16])
        so[0, 128:144] = jnp.concatenate([hi, lo, jnp.zeros((14, GW), bf16)], 0)


def block_of(j, me, nq):
    return jnp.where(j < nq, me[1], 1 - me[1]) * nq + lax.rem(j, nq)


def call_a(me, nm, wx, wy, wb, cw, masks, mrow, hp, rows, di, hd):
    ng = di // GW
    nb = ng + 1
    nq = wx.shape[0]
    own = lambda i, me: block_of(jnp.maximum(i - 1, 0), me, nq)
    col = lambda i, me: (0, jnp.where(i == 0, ng, own(i, me)))
    grp = lambda i, me: (0, own(i, me))
    full = lambda i, me: (0, 0)
    cube = lambda i, me: (0, 0, 0)
    return pl.pallas_call(
        functools.partial(kernel_a, rows, hd, GW // hd, nq),
        grid_spec=pltpu.PrefetchScalarGridSpec(
            num_scalar_prefetch=1,
            grid=(nb,),
            in_specs=[
                pl.BlockSpec(nm.shape, full),
                pl.BlockSpec((1,) + wx.shape[1:], lambda i, me: (jnp.clip(i - 1, 0, nq - 1), 0, 0, 0)),
                pl.BlockSpec((1,) + wx.shape[1:], lambda i, me: (jnp.clip(i - 1 - nq, 0, nq - 1), 0, 0, 0)),
                pl.BlockSpec(wb.shape, cube),
                pl.BlockSpec((8, GW), col),
                pl.BlockSpec((rows, 8), full),
                pl.BlockSpec((8, rows), full),
                pl.BlockSpec((64, 8), full),
            ],
            out_specs=[
                pl.BlockSpec((rows + HALO, GW), col),
                pl.BlockSpec((rows, GW), grp),
                pl.BlockSpec((rows, GW), full),
                pl.BlockSpec((1, 144, GW), lambda i, me: (own(i, me), 0, 0)),
                pl.BlockSpec((64, rows), full),
                pl.BlockSpec((64, rows), full),
                pl.BlockSpec((64, rows), full),
                pl.BlockSpec((9, rows, 128), cube),
            ],
            scratch_shapes=[
                pltpu.VMEM((rows + 8, GW), f32),
                pltpu.VMEM((4, rows, 128), bf16),
                pltpu.VMEM((rows, GW), bf16),
            ],
        ),
        out_shape=[
            jax.ShapeDtypeStruct((rows + HALO, di + GW), bf16),
            jax.ShapeDtypeStruct((rows, di), bf16),
            jax.ShapeDtypeStruct((rows, GW), bf16),
            jax.ShapeDtypeStruct((ng, 144, GW), bf16),
            jax.ShapeDtypeStruct((64, rows), f32),
            jax.ShapeDtypeStruct((64, rows), f32),
            jax.ShapeDtypeStruct((64, rows), f32),
            jax.ShapeDtypeStruct((9, rows, 128), bf16),
        ],
        compiler_params=pltpu.CompilerParams(dimension_semantics=("arbitrary",)),
        cost_estimate=pl.CostEstimate(flops=3000000000, bytes_accessed=12000000, transcendentals=2400000),
        name="conv_state",
    )(me, nm, wx, wy, wb, cw, masks, mrow, hp)


def kernel_f(n, recv, sin, dec):
    state = jnp.zeros((128, GW), f32)
    for i in range(n):
        sin[i] = state.astype(bf16)
        d = recv[i, 128:129].astype(f32) + recv[i, 129:130].astype(f32)
        dec[i] = jnp.broadcast_to(d, (8, GW))
        state = state * d + recv[i, 0:128].astype(f32)


def call_f(recv):
    n = recv.shape[0]
    return pl.pallas_call(
        functools.partial(kernel_f, n),
        out_shape=[
            jax.ShapeDtypeStruct((n, 128, GW), bf16),
            jax.ShapeDtypeStruct((n, 8, GW), f32),
        ],
        name="join_forward",
    )(recv)


def kernel_g(n, recv, dec, gin):
    adj = jnp.zeros((128, GW), f32)
    for i in reversed(range(n)):
        gin[i] = adj.astype(bf16)
        adj = adj * dec[i, 0:1] + recv[i].astype(f32)


def call_g(recv, dec):
    n = recv.shape[0]
    return pl.pallas_call(
        functools.partial(kernel_g, n),
        out_shape=jax.ShapeDtypeStruct((n, 128, GW), bf16),
        name="join_backward",
    )(recv, dec)


def negmask(masks, mrow, c, flip):
    rows = slice(c * LB, (c + 1) * LB)
    same = masks[rows, 3:4] == mrow[4:5, rows]
    a = lax.broadcasted_iota(jnp.int32, (LB, LB), 0)
    b = lax.broadcasted_iota(jnp.int32, (LB, LB), 1)
    order = (a <= b) if flip else (b <= a)
    return jnp.where(same & order, 0.0, NEG)


def half_masks(hd):
    lane = lax.broadcasted_iota(jnp.int32, (LB, 128), 1)
    low = jnp.where(lane < hd, 1.0, 0.0).astype(bf16)
    high = jnp.where(lane < hd, 0.0, 1.0).astype(bf16)
    return low, high


def kernel_b(rows, hd, g0, x, bc, cols, cumt, stept, masks, mrow, yo, score, neg, cumb, st):
    i = pl.program_id(0)
    g = g0 + i
    n = rows // LB

    @pl.when(i == 0)
    def _():
        for c in range(n):
            r = slice(c * LB, (c + 1) * LB)
            score[c] = mm_nt(bc[r, 128:256], bc[r, 0:128])
            neg[c] = negmask(masks, mrow, c, False)

    sel = pick(8 * g, 4 * LB, LB)
    cumb[...] = mm(cols[0], sel) + mm(cols[1], sel) + mm(cols[2], sel)
    sel = pick(8 * g, GW, hd)
    low, high = half_masks(hd)
    for c in range(n):
        r = slice(c * LB, (c + 1) * LB)
        outs = []
        for p in range(2):
            mats = []
            for j in range(2):
                h = 2 * p + j
                diff = cumb[r, h * LB : (h + 1) * LB] - cumt[h : h + 1, r]
                m = jnp.exp(diff + neg[c]) * score[c] * stept[h : h + 1, r]
                mats.append(m.astype(bf16))
            xp = x[r, 128 * p : 128 * (p + 1)]
            outs.append(mm(jnp.concatenate(mats, 1), jnp.concatenate([xp * low, xp * high], 0)))
        y = jnp.concatenate(outs, 1)
        if c > 0:
            w_in = mm(cols[3, r], sel) + mm(cols[4, r], sel)
            y = y + mm(bc[r, 128:256], st[...].astype(bf16)) * w_in
        yo[r] = y
        if c < n - 1:
            w_end = mm(cols[5, r], sel) + mm(cols[6, r], sel)
            fresh = mm_tn(bc[r, 0:128], (x[r].astype(f32) * w_end).astype(bf16))
            if c > 0:
                fresh = fresh + st[...] * w_in[LB - 1 : LB]
            st[...] = fresh


def call_b(x, bc, cols, cumt, stept, masks, mrow, rows, hd, g0, count):
    n = rows // LB
    grp = lambda i: (0, g0 + i)
    row = lambda i: (g0 + i, 0)
    full = lambda i: (0, 0)
    return pl.pallas_call(
        functools.partial(kernel_b, rows, hd, g0),
        grid=(count,),
        in_specs=[
            pl.BlockSpec((rows, GW), grp),
            pl.BlockSpec((rows, GW), full),
            pl.BlockSpec((9, rows, 128), lambda i: (0, 0, 0)),
            pl.BlockSpec((8, rows), row),
            pl.BlockSpec((8, rows), row),
            pl.BlockSpec((rows, 8), full),
            pl.BlockSpec((8, rows), full),
        ],
        out_specs=pl.BlockSpec((rows, GW), lambda i: (0, i)),
        out_shape=jax.ShapeDtypeStruct((rows, count * GW), f32),
        scratch_shapes=[
            pltpu.VMEM((n, LB, LB), f32),
            pltpu.VMEM((n, LB, LB), f32),
            pltpu.VMEM((rows, 4 * LB), f32),
            pltpu.VMEM((128, GW), f32),
        ],
        compiler_params=pltpu.CompilerParams(dimension_semantics=("arbitrary",)),
        cost_estimate=pl.CostEstimate(flops=800000000, bytes_accessed=4000000, transcendentals=1000000),
        name="scan_forward",
    )(x, bc, cols, cumt, stept, masks, mrow)


SR = 16


def kernel_c(ng, hd, ya, yb, x, bc, sin, whi, wlo, gate, gg, skip, gain, gated, gscan, ggate, ggain, go, sel, ys, ws, gw, acc):
    i = pl.program_id(0)
    half = ya.shape[1]
    di = 2 * half

    @pl.when(i == 0)
    def _():
        for g in range(ng):
            sel[:, g * GW : (g + 1) * GW] = pick(8 * g, GW, hd)
        ggain[...] = jnp.zeros_like(ggain)
        acc[...] = jnp.zeros_like(acc)

    for g in range(ng):
        k = slice(g * GW, (g + 1) * GW)
        w = mm(whi[0], sel[:, k]) + mm(wlo[0], sel[:, k])
        ws[:, k] = w
        ys[:, k] = mm(bc[:, 128:256], sin[g]) * w
    inv_di = 1.0 / di

    def body(q, carry):
        r = pl.ds(pl.multiple_of(q * SR, SR), SR)
        local = jnp.concatenate([ya[r, :], yb[r, :]], 1)
        y = local + ys[r, :] + skip[0:1] * x[r, :].astype(f32)
        scanned = y.astype(bf16).astype(f32)
        gt = gate[r, :].astype(f32)
        sg = sigmoid(gt)
        sil = gt * sg
        v = scanned * sil
        ginv = lax.rsqrt(jnp.sum(v * v, 1, keepdims=True) * inv_di + epsilon)
        vn = v * ginv
        gated[r, :] = (vn * gain[0:1]).astype(bf16)
        grad = gg[r, :]
        part = grad * vn
        ggain[0:8] += part[0:8] + part[8:16]
        gl = gain[0:1] * grad
        mean = jnp.sum(gl * v, 1, keepdims=True) * inv_di
        gv = ginv * (gl - v * (ginv * ginv * mean))
        gs = (gv * sil).astype(bf16)
        gscan[r, :] = gs
        ggate[r, :] = (gv * scanned * (sg * (1.0 + gt * (1.0 - sg)))).astype(bf16)
        gw[r, :] = (gs.astype(f32) * ws[r, :]).astype(bf16)
        return carry

    lax.fori_loop(0, LB // SR, body, 0)
    for g in range(ng):
        k = slice(g * GW, (g + 1) * GW)
        acc[g] += mm_tn(bc[:, 128:256], gw[:, k])

    @pl.when(i == pl.num_programs(0) - 1)
    def _():
        go[...] = acc[...].astype(bf16)


def call_c(ya, yb, x, bc, sin, cols, gate, gg, skip, gain, rows, di, hd):
    ng = di // GW
    row = lambda i: (i, 0)
    full = lambda i: (0, 0)
    cube = lambda i: (0, 0, 0)
    wide = pl.BlockSpec((LB, di), row)
    return pl.pallas_call(
        functools.partial(kernel_c, ng, hd),
        grid=(rows // LB,),
        in_specs=[
            pl.BlockSpec((LB, di // 2), row),
            pl.BlockSpec((LB, di // 2), row),
            wide,
            pl.BlockSpec((LB, GW), row),
            pl.BlockSpec((ng, 128, GW), cube),
            pl.BlockSpec((1, LB, 128), lambda i: (7, i, 0)),
            pl.BlockSpec((1, LB, 128), lambda i: (8, i, 0)),
            wide,
            wide,
            pl.BlockSpec((8, di), full),
            pl.BlockSpec((8, di), full),
        ],
        out_specs=[wide, wide, wide, pl.BlockSpec((8, di), full), pl.BlockSpec((ng, 128, GW), cube)],
        out_shape=[
            jax.ShapeDtypeStruct((rows, di), bf16),
            jax.ShapeDtypeStruct((rows, di), bf16),
            jax.ShapeDtypeStruct((rows, di), bf16),
            jax.ShapeDtypeStruct((8, di), f32),
            jax.ShapeDtypeStruct((ng, 128, GW), bf16),
        ],
        scratch_shapes=[
            pltpu.VMEM((128, di), bf16),
            pltpu.VMEM((LB, di), f32),
            pltpu.VMEM((LB, di), f32),
            pltpu.VMEM((LB, di), bf16),
            pltpu.VMEM((ng, 128, GW), f32),
        ],
        compiler_params=pltpu.CompilerParams(dimension_semantics=("arbitrary",)),
        cost_estimate=pl.CostEstimate(flops=1200000000, bytes_accessed=20000000, transcendentals=2000000),
        name="gate_both",
    )(ya, yb, x, bc, sin, cols, cols, gate, gg, skip, gain)


def kernel_d(rows, hd, x, dy, bc, cols, cumt, stept, stepall, masks, mrow, sin, gin, cin, cw, skip, dtt, hp,
             gci, tail, rim, gcw, gdt, hsum,
             score, neg, cumb, stepb, states, zsum, gact, dbc, ext, shifted, arow, crow, grow, xrow, adj):
    i = pl.program_id(0)
    n = rows // LB
    last = pl.num_programs(0) - 1

    @pl.when(i == 0)
    def _():
        for c in range(n):
            r = slice(c * LB, (c + 1) * LB)
            score[c] = mm_nt(bc[r, 0:128], bc[r, 128:256])
            neg[c] = negmask(masks, mrow, c, True)
        zsum[...] = jnp.zeros_like(zsum)
        dbc[...] = jnp.zeros_like(dbc)
        zero = jnp.zeros((8, GW), f32)
        for k in range(TAPS):
            shifted[k, 0:8] = zero
            shifted[k, rows + 8 : rows + 16] = zero

    @pl.when(i < last)
    def _():
        g = i
        sel = pick(8 * g, 4 * LB, LB)
        cumb[...] = mm(cols[0], sel) + mm(cols[1], sel) + mm(cols[2], sel)
        sel = pick(64 + 8 * g, 4 * LB, LB)
        stepb[...] = mm(cols[0], sel) + mm(cols[1], sel) + mm(cols[2], sel)
        sel0 = pick(8 * g, GW, hd)
        sel64 = pick(64 + 8 * g, GW, hd)
        heads = head_rows(hd)
        low, high = half_masks(hd)
        lane = lax.broadcasted_iota(jnp.int32, (LB, 128), 1)
        states[0] = sin[0]
        run = sin[0].astype(f32)
        for c in range(n - 1):
            r = slice(c * LB, (c + 1) * LB)
            e = slice((c + 1) * LB - 16, (c + 1) * LB)
            dec = (mm(cols[3, e], sel0) + mm(cols[4, e], sel0))[15:16]
            w_es = mm(cols[5, r], sel0) + mm(cols[6, r], sel0)
            run = run * dec + mm_tn(bc[r, 0:128], (x[r].astype(f32) * w_es).astype(bf16))
            states[c + 1] = run.astype(bf16)
        adj[...] = gin[0].astype(f32)
        slot = pl.ds(pl.multiple_of(8 * g, 8), 8)
        skipsum = jnp.zeros((1, GW), f32)
        for c in reversed(range(n)):
            r = slice(c * LB, (c + 1) * LB)
            xf = x[r].astype(f32)
            dyf = dy[r].astype(f32)
            b_c, c_c = bc[r, 0:128], bc[r, 128:256]
            w_in = mm(cols[3, r], sel0) + mm(cols[4, r], sel0)
            w_end = mm(cols[3, r], sel64) + mm(cols[4, r], sel64)
            w_es = mm(cols[5, r], sel0) + mm(cols[6, r], sel0)
            st_e = mm(cols[0, r], sel64) + mm(cols[1, r], sel64)
            big = adj[...]
            adj_b = big.astype(bf16)
            st_b = states[c]
            du_out = mm(b_c, adj_b) * w_end
            dbc[r, 0:128] += mm_nt((xf * w_es).astype(bf16), adj_b)
            dyw = dyf * w_in
            dyw_b = dyw.astype(bf16)
            dbc[r, 128:256] += mm_nt(dyw_b, st_b)
            from_state = lane_sums(heads, dyw * mm(c_c, st_b))
            dec = w_in[LB - 1 : LB]
            cross = jnp.sum(big * st_b.astype(f32), 0, keepdims=True) * dec
            cross = lane_sums(heads, jnp.broadcast_to(cross, (LB, GW)))
            adj[...] = big * dec + mm_tn(c_c, dyw_b)
            x_out = lane_sums(heads, xf * du_out)
            zacc = zsum[c]
            pcol = jnp.zeros((LB, 128), f32)
            rsum = []
            dus = []
            for p in range(2):
                k = slice(128 * p, 128 * (p + 1))
                xp, dyp = x[r, k], dy[r, k]
                both = mm_nt(jnp.concatenate([xp * low, xp * high], 0), dyp)
                mats = []
                for j in range(2):
                    h = 2 * p + j
                    hb = slice(h * LB, (h + 1) * LB)
                    diff = cumt[h : h + 1, r] - cumb[r, hb]
                    dmat = jnp.exp(diff + neg[c])
                    kmat = dmat * both[j * LB : (j + 1) * LB]
                    kq = kmat * score[c]
                    sb = stepb[r, hb]
                    zacc = zacc + kmat * sb
                    pcol = jnp.where(lane == h, jnp.sum(kq, 1, keepdims=True), pcol)
                    rsum.append(jnp.sum(kq * sb, 0, keepdims=True))
                    mats.append((dmat * score[c]).astype(bf16))
                dus.append(mm(jnp.concatenate(mats, 1), jnp.concatenate([dyp * low, dyp * high], 0)))
            zsum[c] = zacc
            p_t = pcol.T[0:8]
            rsum = jnp.concatenate(rsum + [jnp.zeros((4, LB), f32)], 0)
            arow[slot, r] = rsum - stept[:, r] * p_t + from_state
            crow[slot, r] = stept[:, r] * x_out
            grow[slot, r] = cross
            xrow[slot, r] = p_t + x_out
            du = jnp.concatenate(dus, 1) + du_out
            gx = st_e * du + skip[0:1] * dyf
            gact[r] = gx.astype(bf16).astype(f32)
            skipsum = skipsum + jnp.sum(xf * dyf, 0, keepdims=True)
        gcw[TAPS + 1 : TAPS + 2] = skipsum

    @pl.when(i == last)
    def _():
        for c in range(n):
            r = slice(c * LB, (c + 1) * LB)
            z = zsum[c].astype(bf16)
            gact[r, 0:128] = dbc[r, 0:128] + mm(z, bc[r, 128:256])
            gact[r, 128:256] = dbc[r, 128:256] + mm_tn(z, bc[r, 0:128])
        rate = jnp.exp(hp[:, 1:2])
        sums = jnp.zeros((64, 1), f32)
        alog = jnp.zeros((64, 1), f32)
        for c in range(n):
            r = slice(c * LB, (c + 1) * LB)
            cr = crow[:, r]
            gl = scan_lanes(arow[:, r], True) + scan_lanes(cr, False) - cr + grow[:, r]
            grad = (xrow[:, r] - rate * gl) * sigmoid(dtt[:, r] + hp[:, 0:1])
            arow[:, r] = grad
            sums = sums + jnp.sum(grad, 1, keepdims=True)
            alog = alog - jnp.sum(gl * (rate * stepall[:, r]), 1, keepdims=True)
        per = GW // hd
        pieces = [arow[8 * g : 8 * g + per] for g in range(8)]
        pieces.append(jnp.zeros((128 - 8 * per, rows), f32))
        gdt[...] = jnp.concatenate(pieces, 0).T.astype(bf16)
        lane = lax.broadcasted_iota(jnp.int32, (64, 128), 1)
        hsum[...] = jnp.where(lane == 0, sums, jnp.where(lane == 1, alog, 0.0))
        gcw[TAPS + 1 : TAPS + 2] = jnp.zeros((1, GW), f32)

    fill_extended(ext, cin, rows)
    parts = [jnp.zeros((8, GW), f32) for _ in range(TAPS + 1)]
    for r in range(0, rows, RC):
        pre = conv_pre(ext, cw, masks, r)
        s = sigmoid(pre)
        gp = gact[r : r + RC] * (s * (1.0 + pre * (1.0 - s)))
        for k in range(TAPS):
            gm = gp if k == TAPS - 1 else gp * masks[r : r + RC, k : k + 1]
            shifted[k, 8 + r : 8 + r + RC] = gm
            off = 8 - (TAPS - 1) + k + r
            prod = gm * ext[off : off + RC]
            for q in range(0, RC, 8):
                parts[k] = parts[k] + prod[q : q + 8]
        for q in range(0, RC, 8):
            parts[TAPS] = parts[TAPS] + gp[q : q + 8]
    for k in range(TAPS + 1):
        gcw[k : k + 1] = jnp.sum(parts[k], 0, keepdims=True)

    def back(start, count):
        total = None
        for k in range(TAPS):
            off = start + TAPS - 1 - k
            term = shifted[k, off : off + count] * cw[k : k + 1]
            total = term if total is None else total + term
        return total

    rim[...] = back(0, 8)
    for r in range(0, rows, RC):
        value = back(8 + r, RC)
        gci[r : r + RC] = value.astype(bf16)
        if r == rows - RC:
            tail[...] = value[RC - HALO : RC]


def call_d(x, dy, bc, cols, cumt, stept, masks, mrow, sin, gin, pc, cw, skip, dtt, hp, rows, di, hd):
    ng = di // GW
    n = rows // LB
    ch = di + GW
    own = lambda i: (0, jnp.minimum(i, ng - 1))
    row = lambda i: (jnp.minimum(i, ng - 1), 0)
    cube = lambda i: (jnp.minimum(i, ng - 1), 0, 0)
    blk = lambda i: (0, i)
    full = lambda i: (0, 0)
    return pl.pallas_call(
        functools.partial(kernel_d, rows, hd),
        grid=(ng + 1,),
        in_specs=[
            pl.BlockSpec((rows, GW), own),
            pl.BlockSpec((rows, GW), own),
            pl.BlockSpec((rows, GW), full),
            pl.BlockSpec((9, rows, 128), lambda i: (0, 0, 0)),
            pl.BlockSpec((8, rows), row),
            pl.BlockSpec((8, rows), row),
            pl.BlockSpec((64, rows), full),
            pl.BlockSpec((rows, 8), full),
            pl.BlockSpec((8, rows), full),
            pl.BlockSpec((1, 128, GW), cube),
            pl.BlockSpec((1, 128, GW), cube),
            pl.BlockSpec((rows + HALO, GW), blk),
            pl.BlockSpec((8, GW), blk),
            pl.BlockSpec((8, GW), own),
            pl.BlockSpec((64, rows), full),
            pl.BlockSpec((64, 8), full),
        ],
        out_specs=[
            pl.BlockSpec((rows, GW), blk),
            pl.BlockSpec((HALO, GW), blk),
            pl.BlockSpec((8, GW), blk),
            pl.BlockSpec((8, GW), blk),
            pl.BlockSpec((rows, 128), full),
            pl.BlockSpec((64, 128), full),
        ],
        out_shape=[
            jax.ShapeDtypeStruct((rows, ch), bf16),
            jax.ShapeDtypeStruct((HALO, ch), f32),
            jax.ShapeDtypeStruct((8, ch), f32),
            jax.ShapeDtypeStruct((8, ch), f32),
            jax.ShapeDtypeStruct((rows, 128), bf16),
            jax.ShapeDtypeStruct((64, 128), f32),
        ],
        scratch_shapes=[
            pltpu.VMEM((n, LB, LB), f32),
            pltpu.VMEM((n, LB, LB), f32),
            pltpu.VMEM((rows, 4 * LB), f32),
            pltpu.VMEM((rows, 4 * LB), f32),
            pltpu.VMEM((n, 128, GW), bf16),
            pltpu.VMEM((n, LB, LB), f32),
            pltpu.VMEM((rows, GW), f32),
            pltpu.VMEM((rows, GW), f32),
            pltpu.VMEM((rows + 8, GW), f32),
            pltpu.VMEM((TAPS, rows + 16, GW), f32),
            pltpu.VMEM((64, rows), f32),
            pltpu.VMEM((64, rows), f32),
            pltpu.VMEM((64, rows), f32),
            pltpu.VMEM((64, rows), f32),
            pltpu.VMEM((128, GW), f32),
        ],
        compiler_params=pltpu.CompilerParams(dimension_semantics=("arbitrary",)),
        cost_estimate=pl.CostEstimate(flops=4000000000, bytes_accessed=14000000, transcendentals=4000000),
        name="scan_backward",
    )(x, dy, bc, cols, cumt, stept, stept, masks, mrow, sin, gin, pc, cw, skip, dtt, hp)


def call_grid(kernel, steps, in_specs, out_specs, out_shape, flops, size, args):
    return pl.pallas_call(
        kernel,
        grid_spec=pltpu.PrefetchScalarGridSpec(num_scalar_prefetch=1, grid=(steps,), in_specs=in_specs, out_specs=out_specs),
        out_shape=out_shape,
        compiler_params=pltpu.CompilerParams(dimension_semantics=("arbitrary",)),
        cost_estimate=pl.CostEstimate(flops=flops, bytes_accessed=size, transcendentals=0),
    )(*args)


def full2(i, me):
    return (0, 0)


def full3(i, me):
    return (0, 0, 0)


def block_xor(j, me, nq):
    return jnp.where(j < nq, me[1], 1 - me[1]) * nq + jnp.bitwise_xor(lax.rem(j, nq), me[0])


def pair_specs(shape, k):
    nq, nw, _, dw, _ = shape
    block = (1, nw, 1, dw, GW)
    mine = pl.BlockSpec(block, lambda i, me: (jnp.minimum(i, nq - 1), 0, k, 0, 0))
    other = pl.BlockSpec(block, lambda i, me: (jnp.maximum(i - nq, 0), 0, k, 0, 0))
    return mine, other


def by_core(me, body, mine, other):
    @pl.when(me[1] == 0)
    def _():
        body(mine, other)

    @pl.when(me[1] == 1)
    def _():
        body(other, mine)


def kernel_gate(nq, me, nm, wx, wy, out):
    i = pl.program_id(0)

    @pl.when(i < nq)
    def _():
        out[...] = mm(nm[...], flat(wx[0, :, 0])).astype(bf16)

    @pl.when(i >= nq)
    def _():
        out[...] = mm(nm[...], flat(wy[0, :, 0])).astype(bf16)


def call_gate(me, nm, wx, wy, di):
    rows = nm.shape[0]
    nq = wx.shape[0]
    specs = [pl.BlockSpec(nm.shape, full2), *pair_specs(wx.shape, 0)]
    out = pl.BlockSpec((rows, GW), lambda i, me: (0, block_xor(i, me, nq)))
    shape = jax.ShapeDtypeStruct((rows, di), bf16)
    flops = 2 * rows * nm.shape[1] * di
    return call_grid(functools.partial(kernel_gate, nq), 2 * nq, specs, out, shape, flops, 8000000, (me, nm, wx, wy))


def kernel_gg(nq, me, cot, wx, wy, out):
    dw = wx.shape[3]

    def body(one, two):
        for c, w in enumerate((one, two)):
            total = None
            for k in range(nq):
                term = mm_nt(cot[jnp.bitwise_xor(me[0], k)], w[k, 0, 0])
                total = term if total is None else total + term
            out[:, c * dw : (c + 1) * dw] = total

    by_core(me, body, wx, wy)


def call_gg(me, cot4, wx, wy, di):
    nq, nw, _, dw, _ = wx.shape
    rows = cot4.shape[1]
    block = pl.BlockSpec((nq, 1, 1, dw, GW), lambda i, me: (0, i, 1, 0, 0))
    specs = [pl.BlockSpec(cot4.shape, full3), block, block]
    out = pl.BlockSpec((rows, 2 * dw), lambda i, me: (0, i))
    shape = jax.ShapeDtypeStruct((rows, di), f32)
    flops = 2 * rows * nq * GW * di
    return call_grid(functools.partial(kernel_gg, nq), nw, specs, out, shape, flops, 10000000, (me, cot4, wx, wy))


def kernel_out(me, gated, wx, wy, x, out):
    nw, dw = wx.shape[1], wx.shape[3]

    def body(one, two):
        total = x[...].astype(f32)
        for k in range(nw):
            for c, w in enumerate((one, two)):
                at = (2 * k + c) * dw
                total = total + mm(gated[:, at : at + dw], w[0, k, 0])
        out[...] = total.astype(bf16)

    by_core(me, body, wx, wy)


def call_out(me, gated, wx, wy, x):
    rows, d = x.shape
    nq, nw, _, dw, _ = wx.shape
    block = pl.BlockSpec((1, nw, 1, dw, GW), lambda i, me: (i, 0, 1, 0, 0))
    cols = pl.BlockSpec((rows, GW), lambda i, me: (0, jnp.bitwise_xor(i, me[0])))
    specs = [pl.BlockSpec(gated.shape, full2), block, block, cols]
    shape = jax.ShapeDtypeStruct((rows, d), bf16)
    return call_grid(kernel_out, nq, specs, cols, shape, 2 * rows * d * gated.shape[1], 8000000, (me, gated, wx, wy, x))


def kernel_pair(me, nt, ggate, gated, cot, keep, send):
    nq, _, _, dw, _ = keep.shape
    first = mm(nt[...], ggate[...])
    second = mm_tn(gated[...], cot[...])

    def body(one, two):
        for c, out in enumerate((one, two)):
            for q in range(nq):
                at = (c * nq + q) * GW
                rel = jnp.bitwise_xor(me[0], q)
                out[rel, 0, 0] = first[:, at : at + GW].astype(bf16)
                out[rel, 0, 1] = second[c * dw : (c + 1) * dw, q * GW : (q + 1) * GW].astype(bf16)

    by_core(me, body, keep, send)


def call_pair(me, nt, ggate, gated, cot, shape):
    nq, nw, _, dw, _ = shape
    rows = cot.shape[0]
    specs = [
        pl.BlockSpec((dw, rows), lambda i, me: (i, 0)),
        pl.BlockSpec(ggate.shape, full2),
        pl.BlockSpec((rows, 2 * dw), lambda i, me: (0, i)),
        pl.BlockSpec(cot.shape, full2),
    ]
    out = [pl.BlockSpec((nq, 1, 2, dw, GW), lambda i, me: (0, i, 0, 0, 0))] * 2
    shapes = [jax.ShapeDtypeStruct(shape, bf16)] * 2
    return call_grid(kernel_pair, nw, specs, out, shapes, 4300000000, 14000000, (me, nt, ggate, gated, cot))


def kernel_late(me, nt, gci, gdt, keep, send):
    nq = keep.shape[0]
    dw = nt.shape[0]
    di = gci.shape[1] - GW
    e = dw // (2 * nq)
    first = mm(nt[...], gci[...])
    dt = mm(nt[...], gdt[...])

    def body(one, two):
        for c, out in enumerate((one, two)):
            for q in range(nq):
                b = c * nq + q
                rel = jnp.bitwise_xor(me[0], q)
                out[rel, 0, 0:dw] = first[:, b * GW : (b + 1) * GW].astype(bf16)
                extra = [first[b * e : (b + 1) * e, di : di + GW]]
                extra.append(jnp.concatenate([dt[b * e : b * e + e // 2], dt[b * e + e // 2 : (b + 1) * e]], 1))
                short = out.shape[2] - dw - e - e // 2
                if short:
                    extra.append(jnp.zeros((short, GW), f32))
                out[rel, 0, dw:] = jnp.concatenate(extra, 0).astype(bf16)

    by_core(me, body, keep, send)


def call_late(me, nt, gci, gdt, shape):
    nq, nw, r, _ = shape
    dw = nt.shape[0] // nw
    specs = [
        pl.BlockSpec((dw, nt.shape[1]), lambda i, me: (i, 0)),
        pl.BlockSpec(gci.shape, full2),
        pl.BlockSpec(gdt.shape, full2),
    ]
    out = [pl.BlockSpec((nq, 1, r, GW), lambda i, me: (0, i, 0, 0))] * 2
    shapes = [jax.ShapeDtypeStruct(shape, bf16)] * 2
    return call_grid(kernel_late, nw, specs, out, shapes, 2500000000, 8000000, (me, nt, gci, gdt))


def kernel_gn_gate(nq, me, g, wx, wy, out):
    i = pl.program_id(0)

    @pl.when(i == 0)
    def _():
        out[...] = jnp.zeros_like(out)

    @pl.when(i < nq)
    def _():
        out[...] += mm_nt(g[...], flat(wx[0, :, 0]))

    @pl.when(i >= nq)
    def _():
        out[...] += mm_nt(g[...], flat(wy[0, :, 0]))


def call_gn_gate(me, g, wx, wy):
    rows = g.shape[0]
    nq, nw, _, dw, _ = wx.shape
    specs = [pl.BlockSpec((rows, GW), lambda i, me: (0, block_xor(i, me, nq))), *pair_specs(wx.shape, 0)]
    out = pl.BlockSpec((rows, nw * dw), full2)
    shape = jax.ShapeDtypeStruct((rows, nw * dw), f32)
    return call_grid(functools.partial(kernel_gn_gate, nq), 2 * nq, specs, out, shape, 2200000000, 8000000, (me, g, wx, wy))


def kernel_gn(nq, me, g, wx, wy, gbc, gdt, wb, start, out):
    i = pl.program_id(0)

    @pl.when(i == 0)
    def _():
        wide = flat(wb[...])
        out[...] = start[...] + mm_nt(gbc[...], wide[:, 0:GW]) + mm_nt(gdt[...], wide[:, GW : GW + 128])

    @pl.when(i < nq)
    def _():
        out[...] += mm_nt(g[...], flat(wx[0]))

    @pl.when(i >= nq)
    def _():
        out[...] += mm_nt(g[...], flat(wy[0]))


def call_gn(me, gci, wx, wy, gdt, wb, start):
    rows = gci.shape[0]
    nq = wx.shape[0]
    block = (1,) + wx.shape[1:]
    specs = [
        pl.BlockSpec((rows, GW), lambda i, me: (0, block_of(i, me, nq))),
        pl.BlockSpec(block, lambda i, me: (jnp.minimum(i, nq - 1), 0, 0, 0)),
        pl.BlockSpec(block, lambda i, me: (jnp.maximum(i - nq, 0), 0, 0, 0)),
        pl.BlockSpec((rows, GW), lambda i, me: (0, 2 * nq)),
        pl.BlockSpec(gdt.shape, full2),
        pl.BlockSpec(wb.shape, full3),
        pl.BlockSpec(start.shape, full2),
    ]
    out = pl.BlockSpec(start.shape, full2)
    shape = jax.ShapeDtypeStruct(start.shape, f32)
    return call_grid(functools.partial(kernel_gn, nq), 2 * nq, specs, out, shape, 2500000000, 12000000, (me, gci, wx, wy, gci, gdt, wb, start))


def slots(values, per):
    groups = values.shape[0] // per
    shaped = values.reshape((groups, per) + values.shape[1:])
    pad = [(0, 0), (0, 8 - per)] + [(0, 0)] * (values.ndim - 1)
    return jnp.pad(shaped, pad).reshape((groups * 8,) + values.shape[1:])


def unslots(values, per):
    groups = values.shape[0] // 8
    return values.reshape((groups, 8) + values.shape[1:])[:, :per].reshape((groups * per,) + values.shape[1:])


SEQ = ("q", "core")


def swap(value, axis):
    return lax.all_to_all(value, axis, split_axis=0, concat_axis=0, tiled=True)


def gather(value, axis):
    return swap(jnp.broadcast_to(value[None], (lax.axis_size(axis),) + value.shape), axis)


def add_up(value, axis):
    return jnp.sum(swap(value, axis).astype(f32), 0).astype(bf16)


def partner(value, axis, k):
    return lax.ppermute(value, axis, [(i, i ^ k) for i in range(lax.axis_size(axis))])


def gather_xor(value, axis):
    return jnp.stack([value] + [partner(value, axis, k) for k in range(1, lax.axis_size(axis))])


def unxor(value, me):
    n = value.shape[0]
    bit = 1
    while bit < n:
        flipped = value.reshape((n // (2 * bit), 2, bit) + value.shape[1:])[:, ::-1].reshape(value.shape)
        value = jnp.where((me & bit) != 0, flipped, value)
        bit *= 2
    return value


def total_of(parts):
    total = parts[0].astype(f32)
    for part in parts[1:]:
        total = total + part.astype(f32)
    return total.astype(bf16)


def reduce_plane(keep, send):
    got = partner(send, "core", 1)
    slots_q = [total_of((keep[k], got[k])) for k in range(keep.shape[0])]
    parts = [slots_q[0]]
    for k in range(1, keep.shape[0]):
        parts.append(partner(slots_q[k], "q", k))
    return total_of(parts)


def layer(x_in, seg_ids, in_weight, out_weight, conv_weight, conv_bias, dt_bias, a_log, skip_gain, norm_gain, gate_gain, cotangent):
    nq, nw = lax.axis_size("q"), lax.axis_size("wsh")
    q_me, c_me = lax.axis_index("q"), lax.axis_index("core")
    nseq = 2 * nq
    rows, d = x_in.shape[1:]
    dw = in_weight.shape[0]
    di = out_weight.shape[0] * nw
    heads = dt_bias.shape[0] * nw
    ch = conv_bias.shape[0] * nw
    hd = di // heads
    per = GW // hd
    ng = di // GW
    x, ids, cot = x_in[0], seg_ids[0], cotangent[0]
    own = c_me * nq + q_me

    forward = [(i, i + 1) for i in range(nseq - 1)]
    x_halo = lax.ppermute(x[rows - HALO :], SEQ, forward)
    id_halo = lax.ppermute(ids[rows - HALO :], SEQ, forward)
    id_halo = jnp.where(q_me + c_me == 0, -1, id_halo)

    x_block = lax.dynamic_slice(in_weight, (0, di + own * GW), (dw, GW))
    gate_block = lax.dynamic_slice(in_weight, (0, own * GW), (dw, GW))
    out_block = lax.dynamic_slice(out_weight, (c_me * dw, q_me * GW), (dw, GW))
    me = jnp.stack([q_me, c_me]).astype(jnp.int32)
    wx0 = gather(gather(x_block, "wsh"), "q")
    wx1 = partner(wx0, "core", 1)
    small = [conv_weight.reshape(-1), conv_bias, dt_bias, a_log, skip_gain, norm_gain, gate_gain]
    sizes = [s.shape[0] for s in small]
    lines = (sum(sizes) + 16 * 384 - 1) // (16 * 384) * 16
    flat_small = jnp.pad(jnp.concatenate(small), (0, lines * 384 - sum(sizes))).reshape(lines, 384)
    bcdt = jnp.pad(in_weight[:, 2 * di :], ((0, 0), (0, 384 - GW - heads)))
    z_b = unxor(gather_xor(jnp.concatenate([bcdt, flat_small], 0), "wsh"), lax.axis_index("wsh"))
    w_b = z_b[:, :dw]
    packed = z_b[:, dw:].reshape(nw, lines * 384)
    go_xor = gather_xor(jnp.stack([gate_block, out_block]), "wsh")
    go_mine = unxor(go_xor, lax.axis_index("wsh"))
    wg0 = gather_xor(go_mine, "q")
    wg1 = partner(wg0, "core", 1)
    cut, at = [], 0
    for s in sizes:
        cut.append(packed[:, at : at + s].astype(f32))
        at += s
    conv_w = cut[0].reshape(nw, TAPS, -1).transpose(1, 0, 2).reshape(TAPS, ch)
    conv_b, dtb, alog, skip_g, norm_g, gate_g = [c.reshape(-1) for c in cut[1:]]
    cw = jnp.concatenate([conv_w, conv_b[None], jnp.zeros((3, ch), f32)], 0)
    hp = jnp.pad(jnp.stack([slots(dtb, per), slots(alog, per)], 1), ((0, 0), (0, 6)))
    skip = jnp.broadcast_to(jnp.repeat(skip_g, hd)[None], (8, di))
    gain = jnp.broadcast_to(gate_g[None], (8, di))

    ext_ids = jnp.concatenate([id_halo[HALO - 3 :], ids])
    prev = id_halo[HALO - 1]
    before = jnp.repeat(jnp.concatenate([prev[None], ids[LB - 1 :: LB][:-1]]), LB)
    ends = jnp.repeat(ids[LB - 1 :: LB], LB)
    zero = jnp.zeros((rows,), f32)
    masks = jnp.stack([(ext_ids[k : k + rows] == ids).astype(f32) for k in range(3)] + [ids.astype(f32)] + [zero] * 4, 1)
    mrow = jnp.stack(
        [(ids == before).astype(f32), (ids == ends).astype(f32), (ids == prev).astype(f32), (ids == ids[rows - 1]).astype(f32), ids.astype(f32)]
        + [zero] * 3,
        0,
    )

    xf = jnp.concatenate([x, x_halo], 0).astype(f32)
    rinv = lax.rsqrt(jnp.mean(xf * xf, 1, keepdims=True) + epsilon)
    normed = (xf * rinv * norm_g[None]).astype(bf16)
    normed_own = normed[:rows]
    normed_t = normed_own.T

    px, xp, bc, s_loc, cumt, stept, dtt, cols = call_a(me, normed, wx0, wx1, w_b, cw, masks, mrow, hp, rows, di, hd)
    recv = swap(s_loc, SEQ)
    ya = call_b(xp, bc, cols, cumt, stept, masks, mrow, rows, hd, 0, ng // 2)
    s_all, dec = call_f(recv)
    s_in = swap(s_all, SEQ)
    yb = call_b(xp, bc, cols, cumt, stept, masks, mrow, rows, hd, ng // 2, ng - ng // 2)

    gate = call_gate(me, normed_own, wg0, wg1, di)
    gg = call_gg(me, cot.reshape(rows, nq, GW).transpose(1, 0, 2), wg0, wg1, di)
    gated, gscan, ggate, ggain, g_loc = call_c(ya, yb, xp, bc, s_in, cols, gate, gg, skip, gain, rows, di, hd)
    g_recv = swap(g_loc, SEQ)
    output = call_out(me, gated, wg0, wg1, x)
    g_all = call_g(g_recv, dec)
    g_in = swap(g_all, SEQ)

    early = call_pair(me, normed_t, ggate, gated, cot, (nq, nw, 2, dw, GW))
    early = add_up(reduce_plane(*early), "wsh")
    early = gather(early, SEQ)
    gn_gate = call_gn_gate(me, ggate, wg0, wg1)

    gci, tail, rim, gcw, gdt, hsum = call_d(
        xp, gscan, bc, cols, cumt, stept, masks, mrow, s_in, g_in, px, cw, skip, dtt, hp, rows, di, hd
    )
    rim_next = lax.ppermute(rim[8 - (TAPS - 1) :], SEQ, [(i + 1, i) for i in range(nseq - 1)])
    fixed = jnp.concatenate([tail[: HALO - (TAPS - 1)], tail[HALO - (TAPS - 1) :] + rim_next], 0)
    gci = lax.dynamic_update_slice(gci, fixed.astype(bf16), (rows - HALO, 0))
    e = dw // nseq
    r_late = dw + (e + e // 2 + 15) // 16 * 16
    late = call_late(me, normed_t, gci, gdt, (nq, nw, r_late, GW))
    late = add_up(reduce_plane(*late), "wsh")
    late = gather(late, SEQ)
    gnorm = call_gn(me, gci, wx0, wx1, gdt, w_b, gn_gate)
    x_own, rinv_own = xf[:rows], rinv[:rows]
    grad_norm = jnp.sum(gnorm * x_own * rinv_own, 0)
    gl = gnorm * norm_g[None]
    mean = jnp.mean(gl * x_own, 1, keepdims=True)
    grad_input = cot.astype(f32) + rinv_own * (gl - x_own * (rinv_own * rinv_own * mean))

    def columns(blocks):
        own_order = blocks.reshape(nq, 2, blocks.shape[1], GW).transpose(2, 1, 0, 3)
        return own_order.reshape(blocks.shape[1], nseq * GW)

    grad_gate = columns(early[:, 0])
    grad_x = columns(late[:, :dw])
    bcdt = late[:, dw:].reshape(nq, 2, r_late - dw, GW).transpose(1, 0, 2, 3)
    grad_bc = bcdt[:, :, :e].reshape(dw, GW)
    grad_dt = bcdt[:, :, e : e + e // 2].reshape(nseq, e // 2, 2, 128).transpose(0, 2, 1, 3).reshape(dw, 128)[:, :heads]
    grad_win = jnp.concatenate([grad_gate, grad_x, grad_bc, grad_dt], 1).astype(f32)
    grad_wout = early[:, 1].reshape(nq, 2, dw, GW).transpose(1, 2, 0, 3).reshape(2 * dw, d).astype(f32)

    pieces = [
        gcw[:TAPS].reshape(TAPS, nw, -1).transpose(1, 0, 2).reshape(nw, -1),
        gcw[TAPS].reshape(nw, -1),
        unslots(hsum[:, 0], per).reshape(nw, -1),
        unslots(hsum[:, 1], per).reshape(nw, -1),
        jnp.sum(gcw[TAPS + 1, :di].reshape(heads, hd), 1).reshape(nw, -1),
        grad_norm.reshape(nw, -1),
        jnp.sum(ggain, 0).reshape(nw, -1),
    ]
    stacked = swap(jnp.concatenate(pieces, 1), "wsh")
    total = jnp.sum(gather(jnp.sum(stacked, 0), SEQ), 0)
    outs, at = [], 0
    for s in sizes:
        outs.append(total[at : at + s])
        at += s
    return (output[None], grad_input[None], grad_win, grad_wout, outs[0].reshape(TAPS, -1)) + tuple(outs[1:])


def solution(mesh):
    nseq, nw = mesh.shape["seq"], mesh.shape["wsh"]
    fine = jax.sharding.Mesh(mesh.devices.reshape(nseq // 2, 2, nw), ("q", "core", "wsh"))
    act, wide, vec = P("wsh", SEQ, None), P("wsh", None), P("wsh")
    in_specs = (act, P("wsh", SEQ), wide, wide, P(None, "wsh"), vec, vec, vec, vec, vec, vec, act)
    out_specs = (act, act, wide, wide, P(None, "wsh"), vec, vec, vec, vec, vec, vec)
    return jax.shard_map(layer, mesh=fine, in_specs=in_specs, out_specs=out_specs, check_vma=False)
```
